32 devices in a mesh: fsdp: 8 (over z, y), ctx: 2 (over x), tp: 2 (over core).
Axes of the slice: x: 2, y: 2, z: 4, core: 2. Of those that a mesh axis runs over, the one named last changes fastest.
Arguments:
- tokens: bfloat16 [3584, 2304], P(('fsdp', 'ctx')), may hold values from -6 to 6
- cotangent: bfloat16 [3584, 2304], P(('fsdp', 'ctx')), may hold values from -6 to 6
- lengths: int32 [8, 1], P('fsdp'), may hold values from 224 to 448, as said below
- positions: int32 [8, 448], P('fsdp'), may hold values from 0 to 447, each once within a row
- query_weight: bfloat16 [2304, 2048], P('fsdp', 'tp'), may hold values from -0.5 to 0.5
- key_weight: bfloat16 [2304, 1024], P('fsdp', 'tp'), may hold values from -0.5 to 0.5
- value_weight: bfloat16 [2304, 1024], P('fsdp', 'tp'), may hold values from -0.125 to 0.125
- output_weight: bfloat16 [2048, 2304], P('tp', 'fsdp'), may hold values from -0.125 to 0.125
- gate_weight: bfloat16 [2304, 9216], P('fsdp', 'tp'), may hold values from -0.125 to 0.125
- up_weight: bfloat16 [2304, 9216], P('fsdp', 'tp'), may hold values from -0.125 to 0.125
- down_weight: bfloat16 [9216, 2304], P('tp', 'fsdp'), may hold values from -0.0625 to 0.0625
- gain_attn_in: bfloat16 [2304], P('fsdp'), may hold values from -0.5 to 0.5
- gain_attn_out: bfloat16 [2304], P('fsdp'), may hold values from -0.5 to 0.5
- gain_ffn_in: bfloat16 [2304], P('fsdp'), may hold values from -0.5 to 0.5
- gain_ffn_out: bfloat16 [2304], P('fsdp'), may hold values from -0.5 to 0.5
Outputs:
- block_out: bfloat16 [3584, 2304], P(('fsdp', 'ctx'))
- tokens_grad: bfloat16 [3584, 2304], P(('fsdp', 'ctx'))
- query_weight_grad: float32 [2304, 2048], P(('fsdp', 'ctx'), 'tp')
- key_weight_grad: float32 [2304, 1024], P(('fsdp', 'ctx'), 'tp')
- value_weight_grad: float32 [2304, 1024], P(('fsdp', 'ctx'), 'tp')
- output_weight_grad: float32 [2048, 2304], P('tp', ('fsdp', 'ctx'))
- gate_weight_grad: float32 [2304, 9216], P(('fsdp', 'ctx'), 'tp')
- up_weight_grad: float32 [2304, 9216], P(('fsdp', 'ctx'), 'tp')
- down_weight_grad: float32 [9216, 2304], P('tp', ('fsdp', 'ctx'))
- gain_attn_in_grad: float32 [2304], P(('fsdp', 'ctx'))
- gain_attn_out_grad: float32 [2304], P(('fsdp', 'ctx'))
- gain_ffn_in_grad: float32 [2304], P(('fsdp', 'ctx'))
- gain_ffn_out_grad: float32 [2304], P(('fsdp', 'ctx'))
The draws below stay inside these ranges and needn't reach their ends.
Inputs may be any that keep to these rules, and one draw needn't show every extreme that they name: lengths[g, 0] is the number of live tokens of group g's sequence; in every draw some group has exactly 448 and another exactly 224. Each row of positions is a permutation of 0 to 447.
All inputs are finite; a program needn't handle non-finite values.
Results may differ from the reference program's by a relative error of at most 0.018.
The reference program's roundings to bfloat16 on the way count: a program that leaves them out, or rounds other values in their place, can miss the bound.
Values may be sent and summed in bfloat16 or wider, within the bound.
No kernel may reach another device: no remote copies, remote signals or barrier semaphores. Data moves between devices by JAX's collectives and lax.ppermute only.
A program may use at most 640 MiB of HBM per device.

```python
import jax
import jax.numpy as jnp
from jax import lax

D = 2304
HEADS = 8
KV_HEADS = 4
HEAD_DIM = 256
FF = 9216
GROUP = 448
TOKENS = 3584
N_FSDP = 8


def draw_lengths(key, part):
    first_key, second_key = jax.random.split(jax.random.fold_in(key, 17))
    base = jax.random.randint(first_key, (N_FSDP, 1), GROUP // 2, GROUP + 1).astype(jnp.int32)
    chosen = jax.random.randint(second_key, (), 0, N_FSDP).astype(jnp.int32)
    rows = jnp.arange(N_FSDP, dtype=jnp.int32)[:, None]
    base = jnp.where(rows == chosen, GROUP, base)
    base = jnp.where(rows == (chosen + 1) % N_FSDP, GROUP // 2, base)
    return base.astype(jnp.int32)


def heavy_head(key):
    return jax.random.randint(jax.random.fold_in(key, 101), (), 0, KV_HEADS).astype(jnp.int32)


def scaled_weight(key, salt, columns, head_of_column):
    chosen = heavy_head(key)
    own_key = jax.random.fold_in(key, salt)
    base = jnp.clip(jax.random.normal(own_key, (D, columns), jnp.float32), -6.0, 6.0)
    factor = jnp.where(head_of_column == chosen, 4.0, 1.0).astype(jnp.float32)
    return base * factor[None, :] * D ** (-0.5)


def draw_query_weight(key, part):
    columns = HEADS * HEAD_DIM
    head_of_column = jnp.arange(columns, dtype=jnp.int32) // HEAD_DIM // (HEADS // KV_HEADS)
    return scaled_weight(key, 211, columns, head_of_column).astype(jnp.bfloat16)


def draw_key_weight(key, part):
    columns = KV_HEADS * HEAD_DIM
    head_of_column = jnp.arange(columns, dtype=jnp.int32) // HEAD_DIM
    return scaled_weight(key, 223, columns, head_of_column).astype(jnp.bfloat16)


def raised(entries, key, source, target, shards_of, factor):
    owner, partner = [(jnp.arange(entries.shape[dim]) // (entries.shape[dim] // shards_of)).reshape([-1 if axis == dim else 1 for axis in range(entries.ndim)]) for dim in (source, target)]
    chosen = jax.random.permutation(key, shards_of)[partner]
    strong = (owner == chosen) | (owner == (partner + shards_of // 2) % shards_of)
    return jnp.where(strong, factor * entries, entries)


def block_scale(key, shape, shards, smallest, largest):
    factor_of = 1.0
    for dim, blocks in shards:
        steps = jax.random.uniform(jax.random.fold_in(jax.random.fold_in(key, 6), dim), (blocks,), jnp.float32, smallest / len(shards), largest / len(shards))
        factor_of = factor_of * jnp.repeat(jnp.exp(steps), shape[dim] // blocks).reshape((-1,) + (1,) * (len(shape) - 1 - dim))
    return factor_of


def noise(stream_key, shape, scale, most, shards=(), held_as=jnp.bfloat16):
    values = scale * jax.random.normal(stream_key, shape, jnp.float32)
    if shards:
        values = values * block_scale(stream_key, shape, shards, -0.22, 0.18)
    return jnp.clip(values, -most, most).astype(held_as)


def heavy_noise(key, shape, width, limit, pieces, heavy, kind=jnp.bfloat16):
    array = width * jax.random.normal(key, shape, jnp.float32)
    if pieces:
        array = array * block_scale(key, shape, pieces, -0.22, 0.18)
    return jnp.clip(raised(array, jax.random.fold_in(key, 3), *heavy), -limit, limit).astype(kind)


def setup_inputs(seed: int = 0) -> dict:
    key_of = jax.random.split(jax.random.key(seed), 16)
    tokens = heavy_noise(key_of[0], (TOKENS, D), 1.0, 6.0, ((0, 16),), (0, 1, 16, 2.0))
    cotangent = heavy_noise(key_of[1], (TOKENS, D), 1.0, 6.0, ((0, 16),), (0, 1, 16, 2.0))
    lengths = draw_lengths(jax.random.fold_in(key_of[15], 71), 0)
    positions = jax.vmap(lambda own: jax.random.permutation(own, GROUP))(jax.random.split(key_of[3], N_FSDP)).reshape((N_FSDP, GROUP)).astype(jnp.int32)
    query_weight = draw_query_weight(jax.random.fold_in(key_of[15], 71), 0)
    key_weight = draw_key_weight(jax.random.fold_in(key_of[15], 71), 0)
    value_weight = noise(key_of[6], (D, KV_HEADS * HEAD_DIM), D ** -0.5, 0.125, ((0, 8), (1, 2)))
    output_weight = noise(key_of[7], (HEADS * HEAD_DIM, D), (HEADS * HEAD_DIM) ** -0.5, 0.125, ((0, 2), (1, 8)))
    gate_weight = noise(key_of[8], (D, FF), D ** -0.5, 0.125, ((0, 8), (1, 2)))
    up_weight = noise(key_of[9], (D, FF), D ** -0.5, 0.125, ((0, 8), (1, 2)))
    down_weight = noise(key_of[10], (FF, D), FF ** -0.5, 0.0625, ((0, 2), (1, 8)))
    gain_attn_in = jnp.clip(jax.random.uniform(key_of[11], (D,), jnp.float32, -0.5, 0.5) * block_scale(key_of[11], (D,), ((0, 8),), -0.4, 0.0), -0.5, 0.5).astype(jnp.bfloat16)
    gain_attn_out = jnp.clip(jax.random.uniform(key_of[12], (D,), jnp.float32, -0.5, 0.5) * block_scale(key_of[12], (D,), ((0, 8),), -0.4, 0.0), -0.5, 0.5).astype(jnp.bfloat16)
    gain_ffn_in = jnp.clip(jax.random.uniform(key_of[13], (D,), jnp.float32, -0.5, 0.5) * block_scale(key_of[13], (D,), ((0, 8),), -0.4, 0.0), -0.5, 0.5).astype(jnp.bfloat16)
    gain_ffn_out = jnp.clip(jax.random.uniform(key_of[14], (D,), jnp.float32, -0.5, 0.5) * block_scale(key_of[14], (D,), ((0, 8),), -0.4, 0.0), -0.5, 0.5).astype(jnp.bfloat16)
    return {"tokens": tokens, "cotangent": cotangent, "lengths": lengths, "positions": positions, "query_weight": query_weight, "key_weight": key_weight, "value_weight": value_weight, "output_weight": output_weight, "gate_weight": gate_weight, "up_weight": up_weight, "down_weight": down_weight, "gain_attn_in": gain_attn_in, "gain_attn_out": gain_attn_out, "gain_ffn_in": gain_ffn_in, "gain_ffn_out": gain_ffn_out}


@jax.custom_vjp
def low(v):
    return lax.optimization_barrier(v.astype(jnp.bfloat16)).astype(jnp.float32)

@jax.custom_vjp
def low_back(v):
    return v

def low_keep(v):
    return (low(v), None)

def low_pass(kept, grad):
    return (grad,)

def back_keep(v):
    return (v, None)

def back_low(kept, grad):
    return (low(grad),)
low.defvjp(low_keep, low_pass)
low_back.defvjp(back_keep, back_low)
eps_norm = 1e-06
soft_cap = 50.0
highest = lax.Precision.HIGHEST

def rms_scale(field, gain_vec):
    factor = lax.rsqrt(lax.optimization_barrier(jnp.mean(field * field, axis=-1, keepdims=True)) + eps_norm)
    return field * factor * (1.0 + gain_vec)

def gelu_tanh(value_in):
    return 0.5 * value_in * (1.0 + jnp.tanh(0.7978845608028654 * (value_in + 0.044715 * value_in * value_in * value_in)))

def placement_of(doc_lengths, packed):
    doc_ends = jnp.cumsum(doc_lengths).astype(jnp.int32)
    after_end = packed[:, None] >= doc_ends[None, :]
    segment = lax.optimization_barrier(jnp.sum(after_end.astype(jnp.int32), axis=1)).astype(jnp.int32)
    inner = (packed - lax.optimization_barrier(jnp.sum(jnp.where(after_end, doc_lengths[None, :], 0), axis=1))).astype(jnp.int32)
    return (segment, inner)

def angles_of(inner, head_size):
    half_size = head_size // 2
    freq = jnp.power(10000.0, -jnp.arange(half_size, dtype=jnp.float32) * (2.0 / head_size))
    return inner.astype(jnp.float32)[:, None] * freq[None, :]

def rotate(field, angles):
    half_size = field.shape[-1] // 2
    cosine = jnp.cos(angles)[:, None, :]
    sine = jnp.sin(angles)[:, None, :]
    first_half = field[..., :half_size]
    second_half = field[..., half_size:]
    return jnp.concatenate([first_half * cosine - second_half * sine, second_half * cosine + first_half * sine], axis=-1)

def layer(resid_in, weights, segment, inner):
    query_w, key_w, value_w, output_w, gate_w, up_w, down_w, gain_one, gain_two, gain_three, gain_four = weights
    group_rows = resid_in.shape[0]
    angles = angles_of(inner, HEAD_DIM)
    normed_attn = low(rms_scale(resid_in, gain_one))
    query_lin = low_back(jnp.dot(normed_attn, query_w, precision=highest)).reshape(group_rows, HEADS, HEAD_DIM)
    key_lin = low_back(jnp.dot(normed_attn, key_w, precision=highest)).reshape(group_rows, KV_HEADS, HEAD_DIM)
    values = low(low_back(jnp.dot(normed_attn, value_w, precision=highest))).reshape(group_rows, KV_HEADS, HEAD_DIM)
    queries = low(rotate(query_lin, angles) * HEAD_DIM ** (-0.5))
    keys = low(rotate(key_lin, angles))
    query_groups = queries.reshape(group_rows, KV_HEADS, HEADS // KV_HEADS, HEAD_DIM)
    raw_scores = low_back(jnp.einsum('qkgd,skd->kgqs', query_groups, keys, precision=highest))
    capped = soft_cap * jnp.tanh(raw_scores / soft_cap)
    allowed = (segment[:, None] == segment[None, :]) & (inner[None, :] <= inner[:, None])
    masked = jnp.where(allowed[None, None], capped, -1e+30)
    row_peak = lax.optimization_barrier(jnp.max(masked, axis=-1, keepdims=True))
    exp_terms = jnp.exp(masked - row_peak)
    probs = exp_terms / lax.optimization_barrier(jnp.sum(exp_terms, axis=-1, keepdims=True))
    probs_low = low(probs)
    attended = low(low_back(jnp.einsum('kgqs,skd->qkgd', probs_low, values, precision=highest))).reshape(group_rows, HEADS * HEAD_DIM)
    attn_out = low_back(jnp.dot(attended, output_w, precision=highest))
    middle = resid_in + rms_scale(attn_out, gain_two)
    normed_ffn = low(rms_scale(middle, gain_three))
    gate_act = low_back(jnp.dot(normed_ffn, gate_w, precision=highest))
    up_act = low_back(jnp.dot(normed_ffn, up_w, precision=highest))
    hidden = low(gelu_tanh(gate_act) * up_act)
    ffn_out = low_back(jnp.dot(hidden, down_w, precision=highest))
    return middle + rms_scale(ffn_out, gain_four)

def reference(tokens, cotangent, lengths, positions, query_weight, key_weight, value_weight, output_weight, gate_weight, up_weight, down_weight, gain_attn_in, gain_attn_out, gain_ffn_in, gain_ffn_out):
    params = tuple((param.astype(jnp.float32) for param in (query_weight, key_weight, value_weight, output_weight, gate_weight, up_weight, down_weight, gain_attn_in, gain_attn_out, gain_ffn_in, gain_ffn_out)))
    tok_groups = tokens.reshape(N_FSDP, GROUP, D)
    cot_groups = cotangent.reshape(N_FSDP, GROUP, D)

    def group_step(totals, items):
        tok_part, cot_part, len_part, pos_part = items
        segment, inner = placement_of(len_part, pos_part)

        def forward(seq_rows, *weights):
            slot_rows = jnp.take(seq_rows, pos_part.astype(jnp.int32), axis=0)
            return layer(slot_rows, weights, segment, inner)
        result, pullback = jax.vjp(forward, tok_part.astype(jnp.float32), *params)
        grads = pullback(cot_part.astype(jnp.float32))
        totals = tuple((running + fresh for running, fresh in zip(totals, grads[1:])))
        return (totals, (result.astype(jnp.bfloat16), grads[0].astype(jnp.bfloat16)))
    zeros_init = tuple((jnp.zeros(param.shape, jnp.float32) for param in params))
    totals, (out_rows, grad_rows) = lax.scan(group_step, zeros_init, (tok_groups, cot_groups, lengths, positions))
    return (out_rows.reshape(TOKENS, D), grad_rows.reshape(TOKENS, D), totals[0], totals[1], totals[2], totals[3], totals[4], totals[5], totals[6], totals[7], totals[8], totals[9], totals[10])
```

```python
import functools

import jax
import jax.numpy as jnp
from jax import lax
from jax.sharding import PartitionSpec as P

HEAD_DIM = 256

eps_norm = 1e-06
soft_cap = 50.0
f32 = jnp.float32
b16 = jnp.bfloat16


def rms_scale(field, gain_vec):
    factor = lax.rsqrt(jnp.mean(field * field, axis=-1, keepdims=True) + eps_norm)
    return field * factor * (1.0 + gain_vec)


def gelu_tanh(value_in):
    return (
        0.5
        * value_in
        * (
            1.0
            + jnp.tanh(0.7978845608028654 * (value_in + 0.044715 * value_in * value_in * value_in))
        )
    )


def glu_apply(gate_act, up_act):
    return gelu_tanh(gate_act) * up_act


def norm_back(field, gain_vec, cot_in):
    pullback = jax.vjp(rms_scale, field, gain_vec)[1]
    return pullback(cot_in)


def placement_of(doc_lengths, packed):
    doc_ends = jnp.cumsum(doc_lengths)
    after_end = packed[:, None] >= doc_ends[None, :]
    segment = jnp.sum(after_end.astype(jnp.int32), axis=1)
    inner = packed - jnp.sum(jnp.where(after_end, doc_lengths[None, :], 0), axis=1)
    return (segment, inner)


def angles_of(inner, head_size):
    half_size = head_size // 2
    freq = jnp.power(10000.0, -jnp.arange(half_size, dtype=f32) * (2.0 / head_size))
    return inner.astype(f32)[:, None] * freq[None, :]


def rotate(field, angles):
    half_size = field.shape[-1] // 2
    cosine = jnp.cos(angles)[:, None, :]
    sine = jnp.sin(angles)[:, None, :]
    first_half = field[..., :half_size]
    second_half = field[..., half_size:]
    return jnp.concatenate(
        [first_half * cosine - second_half * sine, second_half * cosine + first_half * sine],
        axis=-1,
    )


def dot(lhs, rhs, dims):
    return lax.dot_general(lhs, rhs, (dims, ((), ())), preferred_element_type=f32)


def swap(piece, axis):
    return lax.ppermute(piece, axis, [(0, 1), (1, 0)])


def hop(piece, step, n):
    return lax.ppermute(piece, "fsdp", [(d, d ^ step) for d in range(n)])


def gather_rows(own, n):
    have = [own]
    bit = n // 2
    while bit:
        have = have + [hop(piece, bit, n) for piece in have]
        bit //= 2
    mine = jnp.concatenate(have)
    return jnp.concatenate([mine, swap(mine, "tp")])


def scatter_rows(part, n):
    rows = part.shape[0] // (2 * n)
    most = n * rows
    both = part[:most] + swap(part[most:].astype(b16), "tp").astype(f32)
    blocks = [both[k * rows : (k + 1) * rows] for k in range(n)]
    bit = 1
    while bit < n:
        keep = len(blocks) // 2
        blocks = [
            blocks[k] + hop(blocks[keep + k].astype(b16), bit, n).astype(f32) for k in range(keep)
        ]
        bit *= 2
    return blocks[0]


def gather_group(own):
    across = swap(own, "ctx")
    beside = swap(jnp.concatenate([own, across]), "tp")
    rows = own.shape[0]
    return jnp.concatenate([own, beside[:rows], across, beside[rows:]])


def scatter_group(part):
    rows = part.shape[0] // 4
    b0, b1, b2, b3 = [part[k * rows : (k + 1) * rows] for k in range(4)]
    got = swap(jnp.concatenate([b1, b3]), "tp")
    return b0 + got[:rows] + swap(b2 + got[rows:], "ctx")


def natural(own, other, index, axis):
    first = jnp.where(index == 0, own, other)
    second = jnp.where(index == 0, other, own)
    return jnp.concatenate([first, second], axis=axis)


def local(
    n,
    tokens,
    cotangent,
    lengths,
    positions,
    query_weight,
    key_weight,
    value_weight,
    output_weight,
    gate_weight,
    up_weight,
    down_weight,
    gain_attn_in,
    gain_attn_out,
    gain_ffn_in,
    gain_ffn_out,
):
    me = lax.axis_index("fsdp")
    ctx = lax.axis_index("ctx")
    tp = lax.axis_index("tp")
    tok_rows, width = tokens.shape
    rows = tok_rows // 2
    head_size = HEAD_DIM
    d_rows = query_weight.shape[0]
    d_half = d_rows // 2
    q_cols = query_weight.shape[1] // 2
    k_cols = key_weight.shape[1] // 2
    q_local = q_cols // head_size
    kv_local = k_cols // head_size
    group_size = q_local // kv_local
    query_scale = head_size ** (-0.5)
    ff_local = gate_weight.shape[1]
    ff_own = ff_local // n

    starts = [
        c * tok_rows + t * rows for c in (ctx, 1 - ctx) for t in (tp, 1 - tp)
    ]
    packed = jnp.concatenate(
        [lax.dynamic_slice_in_dim(positions[0], start, rows) for start in starts]
    )
    segment, inner = placement_of(lengths[0], packed)
    angles = angles_of(inner, head_size)
    allowed = (segment[:, None] == segment[None, :]) & (inner[None, :] <= inner[:, None])

    mine = lax.dynamic_slice_in_dim(tokens, tp * rows, rows)
    across = swap(mine, "ctx")
    beside = swap(across, "tp")
    seq_group = jnp.concatenate([tokens, across, beside])
    row_ids = jnp.arange(rows, dtype=jnp.int32)
    seq_ids = jnp.concatenate(
        [ctx * tok_rows + jnp.arange(tok_rows, dtype=jnp.int32), starts[2] + row_ids, starts[3] + row_ids]
    )
    pick = (packed[:, None] == seq_ids[None, :]).astype(b16)
    slot_in = dot(pick, seq_group, ((1,), (0,)))
    resid_in = slot_in[:rows]

    qkv_own = jnp.concatenate(
        [
            lax.dynamic_slice_in_dim(query_weight, ctx * q_cols, q_cols, 1),
            lax.dynamic_slice_in_dim(key_weight, ctx * k_cols, k_cols, 1),
            lax.dynamic_slice_in_dim(value_weight, ctx * k_cols, k_cols, 1),
        ],
        axis=1,
    )
    qkv_weight = lax.all_gather(qkv_own, "fsdp", axis=0, tiled=True)
    out_own = lax.dynamic_slice_in_dim(output_weight, ctx * q_cols, q_cols, 0).T
    out_weight = lax.all_gather(out_own, "fsdp", axis=0, tiled=True)
    gains = lax.all_gather(
        jnp.concatenate([gain_attn_in, gain_attn_out, gain_ffn_in, gain_ffn_out])
        .astype(f32)
        .reshape(1, 4 * d_rows),
        "fsdp",
        axis=0,
        tiled=True,
    )
    gains = gains.reshape(n, 4, d_rows).transpose(1, 0, 2).reshape(4, width)

    ffn_own = jnp.stack([gate_weight, up_weight, down_weight.T])
    ffn_own = ffn_own.reshape(3, 2, d_half, n, ff_own).transpose(3, 1, 0, 2, 4)
    ffn_own = lax.dynamic_index_in_dim(ffn_own, ctx, 1, keepdims=False)
    ffn_full = [jnp.zeros((n, 2, d_half, ff_own), b16) for _ in range(3)]
    for k in range(n):
        piece = lax.dynamic_index_in_dim(ffn_own, me ^ k, 0, keepdims=False)
        if k:
            piece = hop(piece, k, n)
        second = swap(piece, "ctx")
        for which in range(3):
            for half, side in ((piece, ctx), (second, 1 - ctx)):
                ffn_full[which] = lax.dynamic_update_slice(
                    ffn_full[which], half[which][None, None], (me ^ k, side, 0, 0)
                )
    gate_full, up_full, down_full = [full.reshape(width, ff_own) for full in ffn_full]

    normed_attn = rms_scale(slot_in, gains[0]).astype(b16)
    qkv = dot(normed_attn, qkv_weight, ((1,), (0,)))
    all_rows = 2 * tok_rows
    query_lin = qkv[:, :q_cols].reshape(all_rows, q_local, head_size)
    key_lin = qkv[:, q_cols : q_cols + k_cols].reshape(all_rows, kv_local, head_size)
    values = qkv[:, q_cols + k_cols :].astype(b16).reshape(all_rows, kv_local, head_size)
    queries = (rotate(query_lin, angles) * query_scale).astype(b16)
    queries = queries.reshape(all_rows, kv_local, group_size, head_size)
    keys = rotate(key_lin, angles).astype(b16)
    raw_scores = jnp.einsum("qkgd,skd->kgqs", queries, keys, preferred_element_type=f32)
    tanh_ratio = jnp.tanh(raw_scores / soft_cap)
    masked = jnp.where(allowed[None, None], soft_cap * tanh_ratio, -1e30)
    row_peak = jnp.max(masked, axis=-1, keepdims=True)
    exp_terms = jnp.exp(masked - row_peak)
    probs = exp_terms / jnp.sum(exp_terms, axis=-1, keepdims=True)
    probs_low = probs.astype(b16)
    attended = (
        jnp.einsum("kgqs,skd->qkgd", probs_low, values, preferred_element_type=f32)
        .reshape(all_rows, q_cols)
        .astype(b16)
    )
    attn_out = scatter_group(dot(attended, out_weight, ((1,), (1,))))
    middle = resid_in + rms_scale(attn_out, gains[1])

    normed_ffn = gather_rows(rms_scale(middle, gains[2]).astype(b16), n)
    gate_act = dot(normed_ffn, gate_full, ((1,), (0,)))
    up_act = dot(normed_ffn, up_full, ((1,), (0,)))
    hidden = glu_apply(gate_act, up_act).astype(b16)
    ffn_out = scatter_rows(dot(hidden, down_full, ((1,), (1,))), n)
    block_own = (middle + rms_scale(ffn_out, gains[3])).astype(b16)
    block_out = natural(block_own, swap(block_own, "tp"), tp, 0)

    d_out = lax.dynamic_slice_in_dim(cotangent, tp * rows, rows).astype(f32)
    d_ffn_raw, gain_four_term = norm_back(ffn_out, gains[3], d_out)
    d_ffn_out = gather_rows(d_ffn_raw.astype(b16), n)
    d_hidden = dot(d_ffn_out, down_full, ((1,), (0,)))
    d_gate_raw, d_up_raw = jax.vjp(glu_apply, gate_act, up_act)[1](d_hidden)
    d_gate = d_gate_raw.astype(b16)
    d_up = d_up_raw.astype(b16)
    d_normed_ffn = scatter_rows(
        dot(d_gate, gate_full, ((1,), (1,))) + dot(d_up, up_full, ((1,), (1,))), n
    )
    ffn_terms = [
        dot(normed_ffn, d_gate, ((0,), (0,))),
        dot(normed_ffn, d_up, ((0,), (0,))),
        dot(d_ffn_out, hidden, ((0,), (0,))),
    ]
    ffn_terms = [term.reshape(n, 2, d_half, ff_own) for term in ffn_terms]
    ffn_keep = [lax.dynamic_index_in_dim(term, ctx, 1, keepdims=False) for term in ffn_terms]
    ffn_send = [
        lax.dynamic_index_in_dim(term, 1 - ctx, 1, keepdims=False).astype(b16)
        for term in ffn_terms
    ]
    ffn_sum = [keep + swap(send, "ctx").astype(f32) for keep, send in zip(ffn_keep, ffn_send)]
    ffn_low = jnp.stack([term.astype(b16) for term in ffn_sum], axis=1)
    ffn_grads = ffn_sum
    for k in range(1, n):
        piece = hop(lax.dynamic_index_in_dim(ffn_low, me ^ k, 0, keepdims=False), k, n)
        ffn_grads = [
            lax.dynamic_update_index_in_dim(grad, piece[which].astype(f32), me ^ k, 0)
            for which, grad in enumerate(ffn_grads)
        ]
    gate_weight_grad = ffn_grads[0].transpose(1, 0, 2).reshape(d_half, ff_local)
    up_weight_grad = ffn_grads[1].transpose(1, 0, 2).reshape(d_half, ff_local)
    down_weight_grad = ffn_grads[2].transpose(0, 2, 1).reshape(ff_local, d_half)

    d_middle_part, gain_three_term = norm_back(middle, gains[2], d_normed_ffn)
    d_middle = d_out + d_middle_part
    d_attn_raw, gain_two_term = norm_back(attn_out, gains[1], d_middle)
    d_attn_out = gather_group(d_attn_raw.astype(b16))
    d_attended = dot(d_attn_out, out_weight, ((1,), (0,))).astype(b16)
    d_att = d_attended.reshape(all_rows, kv_local, group_size, head_size)
    d_probs = jnp.einsum("qkgd,skd->kgqs", d_att, values, preferred_element_type=f32)
    d_soft = probs * (d_probs - jnp.sum(probs * d_probs, axis=-1, keepdims=True))
    d_scores = (d_soft * (1.0 - tanh_ratio * tanh_ratio)).astype(b16)
    d_queries = jnp.einsum("kgqs,skd->qkgd", d_scores, keys, preferred_element_type=f32)
    d_keys = jnp.einsum("kgqs,qkgd->skd", d_scores, queries, preferred_element_type=f32)
    d_values = jnp.einsum("kgqs,qkgd->skd", probs_low, d_att, preferred_element_type=f32)
    d_query_lin = (
        rotate(d_queries.reshape(all_rows, q_local, head_size) * query_scale, -angles)
        .reshape(all_rows, q_cols)
        .astype(b16)
    )
    d_key_lin = rotate(d_keys, -angles).reshape(all_rows, k_cols).astype(b16)
    d_value = d_values.reshape(all_rows, k_cols).astype(b16)
    d_qkv = jnp.concatenate([d_query_lin, d_key_lin, d_value], axis=1)
    d_normed_attn = scatter_group(dot(d_qkv, qkv_weight, ((1,), (1,))))
    resid_part, gain_one_term = norm_back(resid_in, gains[0], d_normed_attn)
    slot_grad = gather_group((d_middle + resid_part).astype(b16))
    place = (
        (ctx * tok_rows + jnp.arange(tok_rows, dtype=jnp.int32))[:, None] == packed[None, :]
    ).astype(b16)
    tokens_grad = dot(place, slot_grad, ((1,), (0,))).astype(b16)

    attn_terms = jnp.concatenate(
        [
            dot(normed_attn, d_qkv, ((0,), (0,))),
            dot(d_attn_out, attended, ((0,), (0,))),
        ],
        axis=1,
    ).astype(b16)
    attn_rows = lax.psum_scatter(attn_terms, "fsdp", scatter_dimension=0, tiled=True)
    attn_rows = attn_rows.reshape(2, d_half, -1)
    attn_own = lax.dynamic_index_in_dim(attn_rows, ctx, 0, keepdims=False)
    attn_other = swap(lax.dynamic_index_in_dim(attn_rows, 1 - ctx, 0, keepdims=False), "ctx")
    edges = [0, q_cols, q_cols + k_cols, q_cols + 2 * k_cols, 2 * q_cols + 2 * k_cols]
    attn_grads = [
        natural(attn_own[:, a:b].astype(f32), attn_other[:, a:b].astype(f32), ctx, 1)
        for a, b in zip(edges[:-1], edges[1:])
    ]

    gain_terms = jnp.stack([gain_one_term, gain_two_term, gain_three_term, gain_four_term])
    gain_terms = gain_terms.reshape(4, 2 * n, d_half).transpose(1, 0, 2).reshape(2 * n, 4 * d_half)
    gain_terms = gain_terms + swap(gain_terms, "tp")
    gain_rows = lax.psum_scatter(gain_terms, ("fsdp", "ctx"), scatter_dimension=0, tiled=True)
    gain_rows = gain_rows.reshape(4, d_half)
    return (
        block_out,
        tokens_grad,
        attn_grads[0],
        attn_grads[1],
        attn_grads[2],
        attn_grads[3].T,
        gate_weight_grad,
        up_weight_grad,
        down_weight_grad,
        gain_rows[0],
        gain_rows[1],
        gain_rows[2],
        gain_rows[3],
    )


def solution(mesh):
    in_specs = (
        P(("fsdp", "ctx"), None),
        P(("fsdp", "ctx"), None),
        P("fsdp", None),
        P("fsdp", None),
        P("fsdp", "tp"),
        P("fsdp", "tp"),
        P("fsdp", "tp"),
        P("tp", "fsdp"),
        P("fsdp", "tp"),
        P("fsdp", "tp"),
        P("tp", "fsdp"),
        P("fsdp"),
        P("fsdp"),
        P("fsdp"),
        P("fsdp"),
    )
    out_specs = (
        P(("fsdp", "ctx"), None),
        P(("fsdp", "ctx"), None),
        P(("fsdp", "ctx"), "tp"),
        P(("fsdp", "ctx"), "tp"),
        P(("fsdp", "ctx"), "tp"),
        P("tp", ("fsdp", "ctx")),
        P(("fsdp", "ctx"), "tp"),
        P(("fsdp", "ctx"), "tp"),
        P("tp", ("fsdp", "ctx")),
        P(("fsdp", "ctx")),
        P(("fsdp", "ctx")),
        P(("fsdp", "ctx")),
        P(("fsdp", "ctx")),
    )
    step = functools.partial(local, mesh.shape["fsdp"])
    return jax.shard_map(step, mesh=mesh, in_specs=in_specs, out_specs=out_specs, check_vma=False)
```

```python
import functools
import math

import jax
import jax.numpy as jnp
from jax import lax
from jax.sharding import PartitionSpec as P

HEAD_DIM = 256

eps_norm = 1e-06
soft_cap = 50.0
f32 = jnp.float32
b16 = jnp.bfloat16


def rms_scale(field, gain_vec):
    factor = lax.rsqrt(jnp.mean(field * field, axis=-1, keepdims=True) + eps_norm)
    return field * factor * (1.0 + gain_vec)


def gelu_tanh(value_in):
    return (
        0.5
        * value_in
        * (
            1.0
            + jnp.tanh(0.7978845608028654 * (value_in + 0.044715 * value_in * value_in * value_in))
        )
    )


def glu_apply(gate_act, up_act):
    return gelu_tanh(gate_act) * up_act


def norm_back(field, gain_vec, cot_in):
    pullback = jax.vjp(rms_scale, field, gain_vec)[1]
    return pullback(cot_in)


def placement_of(doc_lengths, packed):
    doc_ends = jnp.cumsum(doc_lengths)
    after_end = packed[:, None] >= doc_ends[None, :]
    segment = jnp.sum(after_end.astype(jnp.int32), axis=1)
    inner = packed - jnp.sum(jnp.where(after_end, doc_lengths[None, :], 0), axis=1)
    return (segment, inner)


def angles_of(inner, head_size):
    half_size = head_size // 2
    freq = jnp.power(10000.0, -jnp.arange(half_size, dtype=f32) * (2.0 / head_size))
    return inner.astype(f32)[:, None] * freq[None, :]


def rotate(field, angles):
    half_size = field.shape[-1] // 2
    cosine = jnp.cos(angles)[:, None, :]
    sine = jnp.sin(angles)[:, None, :]
    first_half = field[..., :half_size]
    second_half = field[..., half_size:]
    return jnp.concatenate(
        [first_half * cosine - second_half * sine, second_half * cosine + first_half * sine],
        axis=-1,
    )


def dot(lhs, rhs, dims):
    return lax.dot_general(lhs, rhs, (dims, ((), ())), preferred_element_type=f32)


def swap(piece, axis):
    return lax.ppermute(piece, axis, [(0, 1), (1, 0)])


def hop(piece, step, n):
    return lax.ppermute(piece, "fsdp", [(d, d ^ step) for d in range(n)])


def gather_rows(own, n, checks=()):
    have = [own]
    bit = n // 2
    while bit > 1:
        new = [hop(piece, bit, n) for piece in have]
        if bit == n // 2 and checks:
            new = [after(piece, *checks) for piece in new]
        have = have + new
        bit //= 2
    even = jnp.concatenate(have)
    odd = jnp.concatenate([hop(piece, 1, n) for piece in have])
    rows = jnp.concatenate([even, odd, swap(even, "tp"), swap(odd, "tp")])
    return rows, have[-1]


def after(value, *others):
    return lax.optimization_barrier((value, *others))[0]


def scatter_blocks(blocks, bit, n):
    marks = []
    while bit < n:
        keep = len(blocks) // 2
        marks.append(blocks[-1])
        blocks = [
            blocks[k] + hop(blocks[keep + k].astype(b16), bit, n).astype(f32) for k in range(keep)
        ]
        bit *= 2
    return blocks[0], marks


def scatter_rows(product, sources, n):
    most = sources[0].shape[0] // 2
    half = most // 2
    rows = most // n
    ends = [(0, half), (half, most), (most, most + half), (most + half, 2 * most)]
    take = lambda k: product(*[source[ends[k][0] : ends[k][1]] for source in sources])
    far = [swap(take(k).astype(b16), "tp") for k in (3, 2)]
    odd = take(1) + far[0].astype(f32)
    even = take(0) + far[1].astype(f32)
    blocks = [part[k * rows : (k + 1) * rows] for part in (even, odd) for k in range(n // 2)]
    own, marks = scatter_blocks(blocks, 1, n)
    return own, [odd] + marks[1:]


def gather_group(own):
    across = swap(own, "ctx")
    beside = swap(jnp.concatenate([own, across]), "tp")
    rows = own.shape[0]
    return jnp.concatenate([own, beside[:rows], across, beside[rows:]])


def scatter_group(part):
    rows = part.shape[0] // 4
    b0, b1, b2, b3 = [part[k * rows : (k + 1) * rows] for k in range(4)]
    got = swap(jnp.concatenate([b1, b3]), "tp")
    return b0 + got[:rows] + swap((b2 + got[rows:]).astype(b16), "ctx").astype(f32)


def range_order(n):
    order, bit = [0], n // 2
    while bit:
        order = order + [k ^ bit for k in order]
        bit //= 2
    return order


def tile_window(units, n):
    spans = [-(-(d + 1) * units // 128) - d * units // 128 for d in range(n)]
    return 128 * max(spans)


def natural(own, other, index, axis):
    first = jnp.where(index == 0, own, other)
    second = jnp.where(index == 0, other, own)
    return jnp.concatenate([first, second], axis=axis)


def local(
    n,
    tokens,
    cotangent,
    lengths,
    positions,
    query_weight,
    key_weight,
    value_weight,
    output_weight,
    gate_weight,
    up_weight,
    down_weight,
    gain_attn_in,
    gain_attn_out,
    gain_ffn_in,
    gain_ffn_out,
):
    me = lax.axis_index("fsdp")
    ctx = lax.axis_index("ctx")
    tp = lax.axis_index("tp")
    tok_rows, width = tokens.shape
    rows = tok_rows // 2
    head_size = HEAD_DIM
    d_rows = query_weight.shape[0]
    d_half = d_rows // 2
    q_cols = query_weight.shape[1] // 2
    k_cols = key_weight.shape[1] // 2
    q_local = q_cols // head_size
    kv_local = k_cols // head_size
    group_size = q_local // kv_local
    query_scale = head_size ** (-0.5)
    ff_local = gate_weight.shape[1]
    ff_own = ff_local // n

    starts = [
        c * tok_rows + t * rows for c in (ctx, 1 - ctx) for t in (tp, 1 - tp)
    ]
    packed = jnp.concatenate(
        [lax.dynamic_slice_in_dim(positions[0], start, rows) for start in starts]
    )
    segment, inner = placement_of(lengths[0], packed)
    angles = angles_of(inner, head_size)
    allowed = (segment[:, None] == segment[None, :]) & (inner[None, :] <= inner[:, None])

    mine = lax.dynamic_slice_in_dim(tokens, tp * rows, rows)
    across = swap(mine, "ctx")
    beside = swap(across, "tp")
    seq_group = jnp.concatenate([tokens, across, beside])
    row_ids = jnp.arange(rows, dtype=jnp.int32)
    seq_ids = jnp.concatenate(
        [ctx * tok_rows + jnp.arange(tok_rows, dtype=jnp.int32), starts[2] + row_ids, starts[3] + row_ids]
    )
    pick = (packed[:, None] == seq_ids[None, :]).astype(b16)
    slot_in = dot(pick, seq_group, ((1,), (0,)))
    resid_in = slot_in[:rows]

    gain_row = jnp.concatenate([gain_attn_in, gain_attn_out, gain_ffn_in, gain_ffn_out])
    heads_cols = q_cols + 2 * k_cols
    gain_rows = -(-4 * d_rows // heads_cols)
    heads_own = jnp.concatenate(
        [
            lax.dynamic_slice_in_dim(query_weight, ctx * q_cols, q_cols, 1),
            lax.dynamic_slice_in_dim(key_weight, ctx * k_cols, k_cols, 1),
            lax.dynamic_slice_in_dim(value_weight, ctx * k_cols, k_cols, 1),
        ],
        axis=1,
    )
    heads_own = jnp.concatenate(
        [heads_own, jnp.pad(gain_row, (0, 16 * heads_cols - 4 * d_rows)).reshape(16, heads_cols)]
    )
    have = [(0, heads_own)]
    bit = n // 2
    while bit:
        have = have + [(k ^ bit, hop(piece, bit, n)) for k, piece in have]
        bit //= 2
    out_own = lax.dynamic_slice_in_dim(output_weight, ctx * q_cols, q_cols, 0).T
    out_weight = lax.all_gather(out_own, "fsdp", axis=0, tiled=True)
    qkv_weight = jnp.zeros((n, d_rows, heads_cols), b16)
    gains = jnp.zeros((n, gain_rows, heads_cols), b16)
    for k, piece in have:
        put = lambda whole, part: lax.dynamic_update_slice_in_dim(whole, part[None], me ^ k, 0)
        qkv_weight = put(qkv_weight, piece[:d_rows])
        gains = put(gains, piece[d_rows : d_rows + gain_rows])
    qkv_weight = qkv_weight.reshape(width, heads_cols)
    gains = gains.reshape(n, gain_rows * heads_cols)[:, : 4 * d_rows]
    gains = gains.reshape(n, 4, d_rows).transpose(1, 0, 2).reshape(4, width).astype(f32)

    window = tile_window(ff_own, n)
    first = lambda device: (device * ff_own) & -128
    unit = first(me) + jnp.arange(window, dtype=jnp.int32)
    valid = ((unit >= me * ff_own) & (unit < (me + 1) * ff_own))[None]

    def to_units(weights):
        halves = [lax.dynamic_slice_in_dim(weight, ctx * d_half, d_half) for weight in weights]
        own = jnp.stack(
            [
                jnp.concatenate([half[:, first(d) : first(d) + window] for half in halves], axis=1)
                for d in range(n)
            ]
        )
        return lax.all_to_all(own, "fsdp", 0, 0, tiled=True)

    def both_halves(half, other):
        whole = jnp.zeros((n, 2, *half.shape[1:]), b16)
        whole = lax.dynamic_update_slice_in_dim(whole, half[:, None], ctx, 1)
        whole = lax.dynamic_update_slice_in_dim(whole, other[:, None], 1 - ctx, 1)
        return whole.reshape(width, half.shape[2])

    far_piece = have[n // 2 - 1][1]
    gu_half = to_units([after(weight, far_piece) for weight in (gate_weight, up_weight)])

    normed_attn = rms_scale(slot_in, gains[0]).astype(b16)
    qkv = dot(normed_attn, qkv_weight, ((1,), (0,)))
    all_rows = 2 * tok_rows
    query_lin = qkv[:, :q_cols].reshape(all_rows, q_local, head_size)
    key_lin = qkv[:, q_cols : q_cols + k_cols].reshape(all_rows, kv_local, head_size)
    values = qkv[:, q_cols + k_cols :].astype(b16).reshape(all_rows, kv_local, head_size)
    queries = (rotate(query_lin, angles) * query_scale).astype(b16)
    queries = queries.reshape(all_rows, kv_local, group_size, head_size)
    keys = rotate(key_lin, angles).astype(b16)
    raw_scores = jnp.einsum("qkgd,skd->kgqs", queries, keys, preferred_element_type=f32)
    tanh_ratio = jnp.tanh(raw_scores / soft_cap)
    masked = jnp.where(allowed[None, None], soft_cap * tanh_ratio, -1e30)
    row_peak = jnp.max(masked, axis=-1, keepdims=True)
    exp_terms = jnp.exp(masked - row_peak)
    probs = exp_terms / jnp.sum(exp_terms, axis=-1, keepdims=True)
    probs_low = probs.astype(b16)
    attended = (
        jnp.einsum("kgqs,skd->qkgd", probs_low, values, preferred_element_type=f32)
        .reshape(all_rows, q_cols)
        .astype(b16)
    )
    attn_out = scatter_group(dot(attended, out_weight, ((1,), (1,))))
    middle = resid_in + rms_scale(attn_out, gains[1])

    normed_own = rms_scale(middle, gains[2]).astype(b16)
    gu_other = swap(after(gu_half, attn_out), "ctx")
    normed_ffn, mark = gather_rows(normed_own, n)
    down_half = to_units([after(down_weight.T, mark)])
    down_other = swap(after(down_half, gu_other), "ctx")
    gu_full = both_halves(gu_half, gu_other)
    down_full = both_halves(down_half, down_other)
    gate_and_up = dot(normed_ffn, gu_full, ((1,), (0,)))
    gate_act, up_act = gate_and_up[:, :window], gate_and_up[:, window:]
    hidden = jnp.where(valid, glu_apply(gate_act, up_act), 0.0).astype(b16)
    ffn_out, _ = scatter_rows(lambda part: dot(part, down_full, ((1,), (1,))), [hidden], n)
    block_own = (middle + rms_scale(ffn_out, gains[3])).astype(b16)
    block_out = natural(block_own, swap(block_own, "tp"), tp, 0)

    d_out = lax.dynamic_slice_in_dim(cotangent, tp * rows, rows).astype(f32)
    d_ffn_raw, gain_four_term = norm_back(ffn_out, gains[3], d_out)
    d_ffn_out, _ = gather_rows(d_ffn_raw.astype(b16), n)
    d_hidden = dot(d_ffn_out, down_full, ((1,), (0,)))
    d_pair = jax.vjp(glu_apply, gate_act, up_act)[1](d_hidden)
    d_gate, d_up = [jnp.where(valid, part, 0.0).astype(b16) for part in d_pair]
    d_normed_ffn, marks = scatter_rows(
        lambda part: dot(part, gu_full, ((1,), (1,))),
        [jnp.concatenate([d_gate, d_up], axis=1)],
        n,
    )

    def halves(terms):
        terms = terms.reshape(n, 2, d_half, window)
        send = lax.dynamic_index_in_dim(terms, 1 - ctx, 1, keepdims=False).astype(b16)
        return send, lax.dynamic_index_in_dim(terms, ctx, 1, keepdims=False)

    down_send, down_keep = halves(dot(after(d_ffn_out, marks[0]), hidden, ((0,), (0,))))
    late_normed = after(normed_ffn, marks[-1], down_send)
    gate_send, gate_keep = halves(dot(late_normed, d_gate, ((0,), (0,))))
    up_send, up_keep = halves(dot(after(late_normed, gate_send), d_up, ((0,), (0,))))
    down_got, gate_got = swap(down_send, "ctx"), swap(gate_send, "ctx")

    def to_owners(keeps, gots, gate):
        gots = [after(got, gate) for got in gots]
        low = [(keep + got.astype(f32)).astype(b16) for keep, got in zip(keeps, gots)]
        return lax.all_to_all(jnp.concatenate(low, axis=2), "fsdp", 0, 0, tiled=True)

    def columns_joined(whole):
        period = 128 // math.gcd(ff_own, 128)
        tiles = period * ff_own // 128
        parts = whole.reshape(n // period, period, *whole.shape[1:]).astype(f32)
        runs = []
        for tile in range(tiles):
            holds = [
                d
                for d in range(period)
                if d * ff_own < (tile + 1) * 128 and (d + 1) * ff_own > tile * 128
            ]
            if runs and runs[-1][0] == holds and len(holds) == 1:
                runs[-1][2] = tile + 1
            else:
                runs.append([holds, tile, tile + 1])
        pieces = [
            sum(parts[:, d, ..., a * 128 - first(d) : b * 128 - first(d)] for d in holds)
            for holds, a, b in runs
        ]
        joined = jnp.concatenate(pieces, axis=-1)
        return joined.transpose(1, 0, 2).reshape(whole.shape[1], ff_local)

    d_normed_ffn = after(d_normed_ffn, down_got, gate_send, up_send)
    d_middle_part, gain_three_term = norm_back(middle, gains[2], d_normed_ffn)
    d_middle = d_out + d_middle_part
    d_attn_raw, gain_two_term = norm_back(attn_out, gains[1], d_middle)
    d_attn_out = gather_group(d_attn_raw.astype(b16))
    up_got = swap(after(up_send, d_attn_out), "ctx")
    d_attended = dot(d_attn_out, out_weight, ((1,), (0,))).astype(b16)
    dg_rows = to_owners([down_keep, gate_keep], [down_got, gate_got], d_attended)
    d_att = d_attended.reshape(all_rows, kv_local, group_size, head_size)
    d_probs = jnp.einsum("qkgd,skd->kgqs", d_att, values, preferred_element_type=f32)
    d_soft = probs * (d_probs - jnp.sum(probs * d_probs, axis=-1, keepdims=True))
    d_scores = (d_soft * (1.0 - tanh_ratio * tanh_ratio)).astype(b16)
    d_queries = jnp.einsum("kgqs,skd->qkgd", d_scores, keys, preferred_element_type=f32)
    d_keys = jnp.einsum("kgqs,qkgd->skd", d_scores, queries, preferred_element_type=f32)
    d_values = jnp.einsum("kgqs,qkgd->skd", probs_low, d_att, preferred_element_type=f32)
    d_query_lin = (
        rotate(d_queries.reshape(all_rows, q_local, head_size) * query_scale, -angles)
        .reshape(all_rows, q_cols)
        .astype(b16)
    )
    d_key_lin = rotate(d_keys, -angles).reshape(all_rows, k_cols).astype(b16)
    d_value = d_values.reshape(all_rows, k_cols).astype(b16)
    d_qkv = jnp.concatenate([d_query_lin, d_key_lin, d_value], axis=1)
    d_normed_part = dot(d_qkv, qkv_weight, ((1,), (1,)))
    d_normed_attn = scatter_group(d_normed_part)
    resid_part, gain_one_term = norm_back(resid_in, gains[0], d_normed_attn)
    slot_grad = gather_group((d_middle + resid_part).astype(b16))
    unpick = (
        (ctx * tok_rows + jnp.arange(tok_rows, dtype=jnp.int32))[:, None] == packed[None, :]
    ).astype(b16)
    tokens_grad = dot(unpick, slot_grad, ((1,), (0,))).astype(b16)

    attn_terms = [
        dot(normed_attn, d_qkv, ((0,), (0,))).reshape(n, d_rows, -1),
        dot(d_attn_out, attended, ((0,), (0,))).reshape(n, d_rows, -1),
    ]
    attn_rows, marks = scatter_blocks(
        [
            jnp.concatenate(
                [lax.dynamic_index_in_dim(terms, me ^ k, 0, keepdims=False) for terms in attn_terms],
                axis=1,
            )
            for k in range_order(n)
        ],
        1,
        n,
    )
    dg_rows = after(dg_rows, marks[1])
    down_rows, gate_rows = dg_rows[..., :window], dg_rows[..., window:]
    up_rows = to_owners([up_keep], [up_got], dg_rows)
    gate_weight_grad = columns_joined(gate_rows)
    up_weight_grad = columns_joined(up_rows)
    down_weight_grad = columns_joined(down_rows).T
    attn_rows = attn_rows.reshape(2, d_half, -1)
    attn_own = lax.dynamic_index_in_dim(attn_rows, ctx, 0, keepdims=False)
    attn_other = swap(
        lax.dynamic_index_in_dim(attn_rows, 1 - ctx, 0, keepdims=False).astype(b16), "ctx"
    )
    edges = [0, q_cols, q_cols + k_cols, q_cols + 2 * k_cols, 2 * q_cols + 2 * k_cols]
    attn_grads = [
        natural(attn_own[:, a:b].astype(f32), attn_other[:, a:b].astype(f32), ctx, 1)
        for a, b in zip(edges[:-1], edges[1:])
    ]

    gain_terms = jnp.stack([gain_one_term, gain_two_term, gain_three_term, gain_four_term])
    gain_terms = gain_terms + swap(gain_terms, "tp")
    gain_terms = gain_terms.reshape(4, n, 2, d_half).transpose(1, 2, 0, 3)
    gain_terms = lax.dynamic_index_in_dim(gain_terms, ctx, 1, keepdims=False) + swap(
        lax.dynamic_index_in_dim(gain_terms, 1 - ctx, 1, keepdims=False), "ctx"
    )
    gain_rows = jnp.stack(
        [lax.dynamic_index_in_dim(gain_terms, me ^ k, 0, keepdims=False) for k in range_order(n)]
    )
    gain_rows = after(gain_rows, up_rows)
    bit = 1
    while bit < n:
        keep = gain_rows.shape[0] // 2
        gain_rows = gain_rows[:keep] + hop(gain_rows[keep:], bit, n)
        bit *= 2
    gain_rows = gain_rows[0]
    return (
        block_out,
        tokens_grad,
        attn_grads[0],
        attn_grads[1],
        attn_grads[2],
        attn_grads[3].T,
        gate_weight_grad,
        up_weight_grad,
        down_weight_grad,
        gain_rows[0],
        gain_rows[1],
        gain_rows[2],
        gain_rows[3],
    )


def solution(mesh):
    in_specs = (
        P(("fsdp", "ctx"), None),
        P(("fsdp", "ctx"), None),
        P("fsdp", None),
        P("fsdp", None),
        P("fsdp", "tp"),
        P("fsdp", "tp"),
        P("fsdp", "tp"),
        P("tp", "fsdp"),
        P("fsdp", "tp"),
        P("fsdp", "tp"),
        P("tp", "fsdp"),
        P("fsdp"),
        P("fsdp"),
        P("fsdp"),
        P("fsdp"),
    )
    out_specs = (
        P(("fsdp", "ctx"), None),
        P(("fsdp", "ctx"), None),
        P(("fsdp", "ctx"), "tp"),
        P(("fsdp", "ctx"), "tp"),
        P(("fsdp", "ctx"), "tp"),
        P("tp", ("fsdp", "ctx")),
        P(("fsdp", "ctx"), "tp"),
        P(("fsdp", "ctx"), "tp"),
        P("tp", ("fsdp", "ctx")),
        P(("fsdp", "ctx")),
        P(("fsdp", "ctx")),
        P(("fsdp", "ctx")),
        P(("fsdp", "ctx")),
    )
    step = functools.partial(local, mesh.shape["fsdp"])
    return jax.shard_map(step, mesh=mesh, in_specs=in_specs, out_specs=out_specs, check_vma=False)
```

```python
import functools
import math

import jax
import jax.numpy as jnp
from jax import lax
from jax.experimental import pallas as pl
from jax.experimental.pallas import tpu as pltpu
from jax.sharding import PartitionSpec as P

HEAD_DIM = 256

eps_norm = 1e-06
soft_cap = 50.0
f32 = jnp.float32
b16 = jnp.bfloat16


def rms_scale(field, gain_vec):
    factor = lax.rsqrt(jnp.mean(field * field, axis=-1, keepdims=True) + eps_norm)
    return field * factor * (1.0 + gain_vec)


def gelu_tanh(value_in):
    return (
        0.5
        * value_in
        * (
            1.0
            + jnp.tanh(0.7978845608028654 * (value_in + 0.044715 * value_in * value_in * value_in))
        )
    )


def glu_apply(gate_act, up_act):
    return gelu_tanh(gate_act) * up_act


def norm_back(field, gain_vec, cot_in):
    pullback = jax.vjp(rms_scale, field, gain_vec)[1]
    return pullback(cot_in)


def placement_of(doc_lengths, packed):
    doc_ends = jnp.cumsum(doc_lengths)
    after_end = packed[:, None] >= doc_ends[None, :]
    segment = jnp.sum(after_end.astype(jnp.int32), axis=1)
    inner = packed - jnp.sum(jnp.where(after_end, doc_lengths[None, :], 0), axis=1)
    return (segment, inner)


def angles_of(inner, head_size):
    half_size = head_size // 2
    freq = jnp.power(10000.0, -jnp.arange(half_size, dtype=f32) * (2.0 / head_size))
    return inner.astype(f32)[:, None] * freq[None, :]


def turn(field, cosine, sine):
    half = field.shape[1] // 2
    first, second = field[:, :half], field[:, half:]
    return jnp.concatenate(
        [first * cosine - second * sine, second * cosine + first * sine], axis=1
    )


def softmax_of(query, key, allowed):
    ratio = jnp.tanh(dot(query, key, ((1,), (1,))) / soft_cap)
    masked = jnp.where(allowed, soft_cap * ratio, -1e30)
    terms = jnp.exp(masked - jnp.max(masked, axis=1, keepdims=True))
    return ratio, terms / jnp.sum(terms, axis=1, keepdims=True)


def allowed_of(row_ref, col_ref):
    segment, inner = row_ref[:, 0:1], row_ref[:, 1:2]
    return (segment == col_ref[0:1, :]) & (col_ref[1:2, :] <= inner)


def attend_body(heads, kv_heads, qkv_ref, cos_ref, sin_ref, row_ref, col_ref, *out_refs):
    attended_ref, query_ref, key_ref, value_ref = out_refs
    size = HEAD_DIM
    allowed = allowed_of(row_ref, col_ref)
    cosine, sine = cos_ref[...], sin_ref[...]
    for kv in range(kv_heads):
        own = slice(kv * size, (kv + 1) * size)
        at = heads * size + kv * size
        key = turn(qkv_ref[:, at : at + size], cosine, sine).astype(b16)
        at += kv_heads * size
        value = qkv_ref[:, at : at + size].astype(b16)
        key_ref[:, own] = key
        value_ref[:, own] = value
        for head in range(kv * heads // kv_heads, (kv + 1) * heads // kv_heads):
            own = slice(head * size, (head + 1) * size)
            query = (turn(qkv_ref[:, own], cosine, sine) * size**-0.5).astype(b16)
            query_ref[:, own] = query
            _, probs = softmax_of(query, key, allowed)
            attended_ref[:, own] = dot(probs.astype(b16), value, ((1,), (0,))).astype(b16)


def attend_back_body(heads, kv_heads, d_att_ref, query_ref, key_ref, value_ref, cos_ref, sin_ref, row_ref, col_ref, out_ref):
    size = HEAD_DIM
    allowed = allowed_of(row_ref, col_ref)
    cosine, sine = cos_ref[...], sin_ref[...]
    for kv in range(kv_heads):
        own = slice(kv * size, (kv + 1) * size)
        key, value = key_ref[:, own], value_ref[:, own]
        d_key = d_value = 0.0
        for head in range(kv * heads // kv_heads, (kv + 1) * heads // kv_heads):
            own = slice(head * size, (head + 1) * size)
            query, d_att = query_ref[:, own], d_att_ref[:, own]
            ratio, probs = softmax_of(query, key, allowed)
            d_probs = dot(d_att, value, ((1,), (1,)))
            d_soft = probs * (d_probs - jnp.sum(probs * d_probs, axis=1, keepdims=True))
            d_scores = (d_soft * (1.0 - ratio * ratio)).astype(b16)
            d_query = dot(d_scores, key, ((1,), (0,))) * size**-0.5
            out_ref[:, own] = turn(d_query, cosine, -sine).astype(b16)
            d_key += dot(d_scores, query, ((0,), (0,)))
            d_value += dot(probs.astype(b16), d_att, ((0,), (0,)))
        at = heads * size + kv * size
        out_ref[:, at : at + size] = turn(d_key, cosine, -sine).astype(b16)
        at += kv_heads * size
        out_ref[:, at : at + size] = d_value.astype(b16)


def one_block(body, outs, *args):
    return pl.pallas_call(
        body,
        out_shape=outs,
        in_specs=[pl.BlockSpec(memory_space=pltpu.VMEM)] * len(args),
        out_specs=jax.tree.map(lambda _: pl.BlockSpec(memory_space=pltpu.VMEM), outs),
        compiler_params=pltpu.CompilerParams(vmem_limit_bytes=40 << 20),
        cost_estimate=pl.CostEstimate(flops=1000, bytes_accessed=1000, transcendentals=0),
    )(*args)


def dot(lhs, rhs, dims):
    return lax.dot_general(lhs, rhs, (dims, ((), ())), preferred_element_type=f32)


def swap(piece, axis):
    return lax.ppermute(piece, axis, [(0, 1), (1, 0)])


def hop(piece, step, n):
    return lax.ppermute(piece, "fsdp", [(d, d ^ step) for d in range(n)])


def gather_rows(own, n, checks=()):
    have, near = [own], hop(own, 1, n)
    bit = n // 2
    while bit > 1:
        new = [hop(piece, bit, n) for piece in have]
        if len(have) == 1:
            new = [after(new[0], near)]
        have = have + new
        bit //= 2
    even = jnp.concatenate(have)
    odd = jnp.concatenate([near] + [hop(piece, 1, n) for piece in have[1:]])
    rows = jnp.concatenate([even, odd, swap(even, "tp"), swap(odd, "tp")])
    return rows, have[-1]


def after(value, *others):
    return lax.optimization_barrier((value, *others))[0]


def scatter_blocks(blocks, bit, n, serial=False, gates=()):
    marks = []
    while bit < n:
        keep = len(blocks) // 2
        marks.append(blocks[-1])
        came = [None] * keep
        order = sorted(range(keep), key=lambda k: keys_of(n)[k], reverse=True)
        for at, k in enumerate(order):
            piece = blocks[keep + k].astype(b16)
            if serial and bit == 1 and at:
                piece = after(piece, came[order[at - 1]], *(gates if at == 1 else ()))
            came[k] = hop(piece, bit, n)
            if serial and bit == 1 and at == 1:
                marks[0] = came[k]
        blocks = [block + piece.astype(f32) for block, piece in zip(blocks, came)]
        bit *= 2
    return blocks[0], marks


def scatter_rows(product, sources, n):
    most = sources[0].shape[0] // 2
    half = most // 2
    rows = most // n
    ends = [(0, half), (half, most), (most, most + half), (most + half, 2 * most)]
    take = lambda k: product(*[source[ends[k][0] : ends[k][1]] for source in sources])
    far = [swap(take(k).astype(b16), "tp") for k in (3, 2)]
    odd = take(1) + far[0].astype(f32)
    even = take(0) + far[1].astype(f32)
    blocks = [part[k * rows : (k + 1) * rows] for part in (even, odd) for k in range(n // 2)]
    own, marks = scatter_blocks(blocks, 1, n)
    return own, [odd] + marks[1:]


def gather_group(own):
    across = swap(own, "ctx")
    beside = swap(jnp.concatenate([own, across]), "tp")
    rows = own.shape[0]
    return jnp.concatenate([own, beside[:rows], across, beside[rows:]])


def scatter_group(part):
    rows = part.shape[0] // 4
    b0, b1, b2, b3 = [part[k * rows : (k + 1) * rows] for k in range(4)]
    got = swap(jnp.concatenate([b1, b3]), "tp")
    return b0 + got[:rows] + swap((b2 + got[rows:]).astype(b16), "ctx").astype(f32)


def keys_of(n):
    order, bit = [0], n // 2
    while bit:
        order = order + [k ^ bit for k in order]
        bit //= 2
    return order


def tile_window(units, n):
    spans = [-(-(d + 1) * units // 128) - d * units // 128 for d in range(n)]
    return 128 * max(spans)


def natural(own, other, index, axis):
    first = jnp.where(index == 0, own, other)
    second = jnp.where(index == 0, other, own)
    return jnp.concatenate([first, second], axis=axis)


def local(
    n,
    tokens,
    cotangent,
    lengths,
    positions,
    query_weight,
    key_weight,
    value_weight,
    output_weight,
    gate_weight,
    up_weight,
    down_weight,
    gain_attn_in,
    gain_attn_out,
    gain_ffn_in,
    gain_ffn_out,
):
    me = lax.axis_index("fsdp")
    ctx = lax.axis_index("ctx")
    tp = lax.axis_index("tp")
    tok_rows, width = tokens.shape
    rows = tok_rows // 2
    head_size = HEAD_DIM
    d_rows = query_weight.shape[0]
    d_half = d_rows // 2
    q_cols = query_weight.shape[1] // 2
    k_cols = key_weight.shape[1] // 2
    q_local = q_cols // head_size
    kv_local = k_cols // head_size
    ff_local = gate_weight.shape[1]
    ff_own = ff_local // n

    starts = [
        c * tok_rows + t * rows for c in (ctx, 1 - ctx) for t in (tp, 1 - tp)
    ]
    packed = jnp.concatenate(
        [lax.dynamic_slice_in_dim(positions[0], start, rows) for start in starts]
    )
    segment, inner = placement_of(lengths[0], packed)
    angles = angles_of(inner, head_size)

    mine = lax.dynamic_slice_in_dim(tokens, tp * rows, rows)
    across = swap(mine, "ctx")
    beside = swap(across, "tp")
    seq_group = jnp.concatenate([tokens, across, beside])
    row_ids = jnp.arange(rows, dtype=jnp.int32)
    seq_ids = jnp.concatenate(
        [ctx * tok_rows + jnp.arange(tok_rows, dtype=jnp.int32), starts[2] + row_ids, starts[3] + row_ids]
    )
    pick = (packed[:, None] == seq_ids[None, :]).astype(b16)
    slot_in = dot(pick, seq_group, ((1,), (0,)))
    resid_in = slot_in[:rows]

    gain_row = jnp.concatenate([gain_attn_in, gain_attn_out, gain_ffn_in, gain_ffn_out])
    heads_cols = q_cols + 2 * k_cols
    gain_rows = -(-4 * d_rows // heads_cols)
    heads_own = jnp.concatenate(
        [
            lax.dynamic_slice_in_dim(query_weight, ctx * q_cols, q_cols, 1),
            lax.dynamic_slice_in_dim(key_weight, ctx * k_cols, k_cols, 1),
            lax.dynamic_slice_in_dim(value_weight, ctx * k_cols, k_cols, 1),
        ],
        axis=1,
    )
    heads_own = jnp.concatenate(
        [heads_own, jnp.pad(gain_row, (0, 16 * heads_cols - 4 * d_rows)).reshape(16, heads_cols)]
    )
    have = [(0, heads_own)]
    bit = n // 2
    while bit:
        have = have + [(k ^ bit, hop(piece, bit, n)) for k, piece in have]
        bit //= 2
    out_own = lax.dynamic_slice_in_dim(output_weight, ctx * q_cols, q_cols, 0).T
    out_weight = lax.all_gather(out_own, "fsdp", axis=0, tiled=True)
    qkv_weight = jnp.zeros((n, d_rows, heads_cols), b16)
    gains = jnp.zeros((n, gain_rows, heads_cols), b16)
    for k, piece in have:
        put = lambda whole, part: lax.dynamic_update_slice_in_dim(whole, part[None], me ^ k, 0)
        qkv_weight = put(qkv_weight, piece[:d_rows])
        gains = put(gains, piece[d_rows : d_rows + gain_rows])
    qkv_weight = qkv_weight.reshape(width, heads_cols)
    gains = gains.reshape(n, gain_rows * heads_cols)[:, : 4 * d_rows]
    gains = gains.reshape(n, 4, d_rows).transpose(1, 0, 2).reshape(4, width).astype(f32)

    window = tile_window(ff_own, n)
    first = lambda device: (device * ff_own) & -128
    unit = first(me) + jnp.arange(window, dtype=jnp.int32)
    valid = ((unit >= me * ff_own) & (unit < (me + 1) * ff_own))[None]

    def to_units(weights):
        halves = [lax.dynamic_slice_in_dim(weight, ctx * d_half, d_half) for weight in weights]
        own = jnp.stack(
            [
                jnp.concatenate([half[:, first(d) : first(d) + window] for half in halves], axis=1)
                for d in range(n)
            ]
        )
        return lax.all_to_all(own, "fsdp", 0, 0, tiled=True)

    def both_halves(half, other):
        whole = jnp.zeros((n, 2, *half.shape[1:]), b16)
        whole = lax.dynamic_update_slice_in_dim(whole, half[:, None], ctx, 1)
        whole = lax.dynamic_update_slice_in_dim(whole, other[:, None], 1 - ctx, 1)
        return whole.reshape(width, half.shape[2])

    far_piece = have[n // 2 - 1][1]
    gu_half = to_units([after(weight, far_piece) for weight in (gate_weight, up_weight)])

    normed_attn = rms_scale(slot_in, gains[0]).astype(b16)
    qkv = dot(normed_attn, qkv_weight, ((1,), (0,)))
    all_rows = 2 * tok_rows
    cosine, sine = jnp.cos(angles), jnp.sin(angles)
    places = jnp.stack([segment, inner])
    held = lambda cols: jax.ShapeDtypeStruct((all_rows, cols), b16)
    attended, queries, keys, values = one_block(
        functools.partial(attend_body, q_local, kv_local),
        [held(q_cols), held(q_cols), held(k_cols), held(k_cols)],
        qkv,
        cosine,
        sine,
        places.T,
        places,
    )
    attn_out = scatter_group(dot(attended, out_weight, ((1,), (1,))))
    middle = resid_in + rms_scale(attn_out, gains[1])

    normed_own = rms_scale(middle, gains[2]).astype(b16)
    gu_other = swap(after(gu_half, attn_out), "ctx")
    normed_ffn, mark = gather_rows(normed_own, n)
    down_half = to_units([after(down_weight.T, mark)])
    down_other = swap(after(down_half, gu_other), "ctx")
    gu_full = both_halves(gu_half, gu_other)
    down_full = both_halves(down_half, down_other)
    gate_and_up = dot(normed_ffn, gu_full, ((1,), (0,)))
    gate_act, up_act = gate_and_up[:, :window], gate_and_up[:, window:]
    hidden = jnp.where(valid, glu_apply(gate_act, up_act), 0.0).astype(b16)
    ffn_out, _ = scatter_rows(lambda part: dot(part, down_full, ((1,), (1,))), [hidden], n)
    block_own = (middle + rms_scale(ffn_out, gains[3])).astype(b16)
    block_out = natural(block_own, swap(block_own, "tp"), tp, 0)

    d_out = lax.dynamic_slice_in_dim(cotangent, tp * rows, rows).astype(f32)
    d_ffn_raw, gain_four_term = norm_back(ffn_out, gains[3], d_out)
    d_ffn_out, _ = gather_rows(d_ffn_raw.astype(b16), n)
    d_hidden = dot(d_ffn_out, down_full, ((1,), (0,)))
    d_pair = jax.vjp(glu_apply, gate_act, up_act)[1](d_hidden)
    d_gate, d_up = [jnp.where(valid, part, 0.0).astype(b16) for part in d_pair]
    d_normed_ffn, marks = scatter_rows(
        lambda part: dot(part, gu_full, ((1,), (1,))),
        [jnp.concatenate([d_gate, d_up], axis=1)],
        n,
    )

    def halves(terms):
        terms = terms.reshape(n, 2, d_half, window)
        send = lax.dynamic_index_in_dim(terms, 1 - ctx, 1, keepdims=False).astype(b16)
        return send, lax.dynamic_index_in_dim(terms, ctx, 1, keepdims=False)

    down_send, down_keep = halves(dot(after(d_ffn_out, marks[0]), hidden, ((0,), (0,))))
    late_normed = after(normed_ffn, marks[-1], down_send)
    gate_send, gate_keep = halves(dot(late_normed, d_gate, ((0,), (0,))))
    up_send, up_keep = halves(dot(after(late_normed, gate_send), d_up, ((0,), (0,))))
    down_got, gate_got = swap(down_send, "ctx"), swap(gate_send, "ctx")

    def to_owners(keeps, gots, gate):
        gots = [after(got, gate) for got in gots]
        low = [(keep + got.astype(f32)).astype(b16) for keep, got in zip(keeps, gots)]
        return lax.all_to_all(jnp.concatenate(low, axis=2), "fsdp", 0, 0, tiled=True)

    def columns_joined(whole):
        period = 128 // math.gcd(ff_own, 128)
        tiles = period * ff_own // 128
        parts = whole.reshape(n // period, period, *whole.shape[1:]).astype(f32)
        runs = []
        for tile in range(tiles):
            holds = [
                d
                for d in range(period)
                if d * ff_own < (tile + 1) * 128 and (d + 1) * ff_own > tile * 128
            ]
            if runs and runs[-1][0] == holds and len(holds) == 1:
                runs[-1][2] = tile + 1
            else:
                runs.append([holds, tile, tile + 1])
        pieces = [
            sum(parts[:, d, ..., a * 128 - first(d) : b * 128 - first(d)] for d in holds)
            for holds, a, b in runs
        ]
        joined = jnp.concatenate(pieces, axis=-1)
        return joined.transpose(1, 0, 2).reshape(whole.shape[1], ff_local)

    d_normed_ffn = after(d_normed_ffn, down_got, gate_send, up_send)
    d_middle_part, gain_three_term = norm_back(middle, gains[2], d_normed_ffn)
    d_middle = d_out + d_middle_part
    d_attn_raw, gain_two_term = norm_back(attn_out, gains[1], d_middle)
    d_attn_out = gather_group(d_attn_raw.astype(b16))
    up_got = swap(after(up_send, d_attn_out), "ctx")
    down_rows = to_owners([down_keep], [down_got], d_normed_ffn)
    d_attended = dot(d_attn_out, out_weight, ((1,), (0,))).astype(b16)
    d_qkv = one_block(
        functools.partial(attend_back_body, q_local, kv_local),
        held(q_cols + 2 * k_cols),
        d_attended,
        queries,
        keys,
        values,
        cosine,
        sine,
        places.T,
        places,
    )
    d_normed_part = dot(d_qkv, qkv_weight, ((1,), (1,)))
    d_normed_attn = scatter_group(d_normed_part)
    resid_part, gain_one_term = norm_back(resid_in, gains[0], d_normed_attn)
    slot_grad = gather_group((d_middle + resid_part).astype(b16))
    unpick = (
        (ctx * tok_rows + jnp.arange(tok_rows, dtype=jnp.int32))[:, None] == packed[None, :]
    ).astype(b16)
    tokens_grad = dot(unpick, slot_grad, ((1,), (0,))).astype(b16)

    attn_terms = [
        dot(normed_attn, d_qkv, ((0,), (0,))).reshape(n, d_rows, -1),
        dot(d_attn_out, attended, ((0,), (0,))).reshape(n, d_rows, -1),
    ]
    attn_rows, marks = scatter_blocks(
        [
            jnp.concatenate(
                [lax.dynamic_index_in_dim(terms, me ^ k, 0, keepdims=False) for terms in attn_terms],
                axis=1,
            )
            for k in keys_of(n)
        ],
        1,
        n,
        serial=True,
        gates=[down_rows],
    )
    gu_rows = after(to_owners([gate_keep, up_keep], [gate_got, up_got], marks[0]), attn_rows)
    gate_rows, up_rows = gu_rows[..., :window], gu_rows[..., window:]
    gate_weight_grad = columns_joined(gate_rows)
    up_weight_grad = columns_joined(up_rows)
    down_weight_grad = columns_joined(down_rows).T
    attn_rows = attn_rows.reshape(2, d_half, -1)
    attn_own = lax.dynamic_index_in_dim(attn_rows, ctx, 0, keepdims=False)
    attn_other = swap(
        lax.dynamic_index_in_dim(attn_rows, 1 - ctx, 0, keepdims=False).astype(b16), "ctx"
    )
    edges = [0, q_cols, q_cols + k_cols, q_cols + 2 * k_cols, 2 * q_cols + 2 * k_cols]
    attn_grads = [
        natural(attn_own[:, a:b].astype(f32), attn_other[:, a:b].astype(f32), ctx, 1)
        for a, b in zip(edges[:-1], edges[1:])
    ]

    gain_terms = jnp.stack([gain_one_term, gain_two_term, gain_three_term, gain_four_term])
    gain_terms = gain_terms + swap(gain_terms, "tp")
    gain_terms = gain_terms.reshape(4, n, 2, d_half).transpose(1, 2, 0, 3)
    gain_terms = lax.dynamic_index_in_dim(gain_terms, ctx, 1, keepdims=False) + swap(
        lax.dynamic_index_in_dim(gain_terms, 1 - ctx, 1, keepdims=False), "ctx"
    )
    gain_rows = jnp.stack(
        [lax.dynamic_index_in_dim(gain_terms, me ^ k, 0, keepdims=False) for k in keys_of(n)]
    )
    gain_rows = after(gain_rows, attn_rows)
    bit = 1
    while bit < n:
        keep = gain_rows.shape[0] // 2
        gain_rows = gain_rows[:keep] + hop(gain_rows[keep:], bit, n)
        bit *= 2
    gain_rows = gain_rows[0]
    return (
        block_out,
        tokens_grad,
        attn_grads[0],
        attn_grads[1],
        attn_grads[2],
        attn_grads[3].T,
        gate_weight_grad,
        up_weight_grad,
        down_weight_grad,
        gain_rows[0],
        gain_rows[1],
        gain_rows[2],
        gain_rows[3],
    )


def solution(mesh):
    in_specs = (
        P(("fsdp", "ctx"), None),
        P(("fsdp", "ctx"), None),
        P("fsdp", None),
        P("fsdp", None),
        P("fsdp", "tp"),
        P("fsdp", "tp"),
        P("fsdp", "tp"),
        P("tp", "fsdp"),
        P("fsdp", "tp"),
        P("fsdp", "tp"),
        P("tp", "fsdp"),
        P("fsdp"),
        P("fsdp"),
        P("fsdp"),
        P("fsdp"),
    )
    out_specs = (
        P(("fsdp", "ctx"), None),
        P(("fsdp", "ctx"), None),
        P(("fsdp", "ctx"), "tp"),
        P(("fsdp", "ctx"), "tp"),
        P(("fsdp", "ctx"), "tp"),
        P("tp", ("fsdp", "ctx")),
        P(("fsdp", "ctx"), "tp"),
        P(("fsdp", "ctx"), "tp"),
        P("tp", ("fsdp", "ctx")),
        P(("fsdp", "ctx")),
        P(("fsdp", "ctx")),
        P(("fsdp", "ctx")),
        P(("fsdp", "ctx")),
    )
    step = functools.partial(local, mesh.shape["fsdp"])
    return jax.shard_map(step, mesh=mesh, in_specs=in_specs, out_specs=out_specs, check_vma=False)
```

```python
import functools
import math

import jax
import jax.numpy as jnp
from jax import lax
from jax.experimental import pallas as pl
from jax.experimental.pallas import tpu as pltpu
from jax.sharding import PartitionSpec as P

HEAD_DIM = 256

eps_norm = 1e-06
soft_cap = 50.0
f32 = jnp.float32
b16 = jnp.bfloat16


def rms_scale(field, gain_vec):
    factor = lax.rsqrt(jnp.mean(field * field, axis=-1, keepdims=True) + eps_norm)
    return field * factor * (1.0 + gain_vec)


def gelu_tanh(value_in):
    return (
        0.5
        * value_in
        * (
            1.0
            + jnp.tanh(0.7978845608028654 * (value_in + 0.044715 * value_in * value_in * value_in))
        )
    )


def glu_apply(gate_act, up_act):
    return gelu_tanh(gate_act) * up_act


def norm_back(field, gain_vec, cot_in):
    pullback = jax.vjp(rms_scale, field, gain_vec)[1]
    return pullback(cot_in)


def placement_of(doc_lengths, packed):
    doc_ends = jnp.cumsum(doc_lengths)
    after_end = packed[:, None] >= doc_ends[None, :]
    segment = jnp.sum(after_end.astype(jnp.int32), axis=1)
    inner = packed - jnp.sum(jnp.where(after_end, doc_lengths[None, :], 0), axis=1)
    return (segment, inner)


def angles_of(inner, head_size):
    half_size = head_size // 2
    freq = jnp.power(10000.0, -jnp.arange(half_size, dtype=f32) * (2.0 / head_size))
    return inner.astype(f32)[:, None] * freq[None, :]


def turn(field, cosine, sine):
    half = field.shape[1] // 2
    first, second = field[:, :half], field[:, half:]
    return jnp.concatenate(
        [first * cosine - second * sine, second * cosine + first * sine], axis=1
    )


def softmax_of(query, key, allowed):
    ratio = jnp.tanh(dot(query, key, ((1,), (1,))) / soft_cap)
    masked = jnp.where(allowed, soft_cap * ratio, -1e30)
    terms = jnp.exp(masked - jnp.max(masked, axis=1, keepdims=True))
    return ratio, terms / jnp.sum(terms, axis=1, keepdims=True)


def allowed_of(row_ref, col_ref):
    segment, inner = row_ref[:, 0:1], row_ref[:, 1:2]
    return (segment == col_ref[0:1, :]) & (col_ref[1:2, :] <= inner)


def attend_body(heads, kv_heads, qkv_ref, cos_ref, sin_ref, row_ref, col_ref, *out_refs):
    attended_ref, query_ref, key_ref, value_ref = out_refs
    size = HEAD_DIM
    allowed = allowed_of(row_ref, col_ref)
    cosine, sine = cos_ref[...], sin_ref[...]
    for kv in range(kv_heads):
        own = slice(kv * size, (kv + 1) * size)
        at = heads * size + kv * size
        key = turn(qkv_ref[:, at : at + size], cosine, sine).astype(b16)
        at += kv_heads * size
        value = qkv_ref[:, at : at + size].astype(b16)
        key_ref[:, own] = key
        value_ref[:, own] = value
        for head in range(kv * heads // kv_heads, (kv + 1) * heads // kv_heads):
            own = slice(head * size, (head + 1) * size)
            query = (turn(qkv_ref[:, own], cosine, sine) * size**-0.5).astype(b16)
            query_ref[:, own] = query
            _, probs = softmax_of(query, key, allowed)
            attended_ref[:, own] = dot(probs.astype(b16), value, ((1,), (0,))).astype(b16)


def attend_back_body(heads, kv_heads, d_att_ref, query_ref, key_ref, value_ref, cos_ref, sin_ref, row_ref, col_ref, out_ref):
    size = HEAD_DIM
    allowed = allowed_of(row_ref, col_ref)
    cosine, sine = cos_ref[...], sin_ref[...]
    for kv in range(kv_heads):
        own = slice(kv * size, (kv + 1) * size)
        key, value = key_ref[:, own], value_ref[:, own]
        d_key = d_value = 0.0
        for head in range(kv * heads // kv_heads, (kv + 1) * heads // kv_heads):
            own = slice(head * size, (head + 1) * size)
            query, d_att = query_ref[:, own], d_att_ref[:, own]
            ratio, probs = softmax_of(query, key, allowed)
            d_probs = dot(d_att, value, ((1,), (1,)))
            d_soft = probs * (d_probs - jnp.sum(probs * d_probs, axis=1, keepdims=True))
            d_scores = (d_soft * (1.0 - ratio * ratio)).astype(b16)
            d_query = dot(d_scores, key, ((1,), (0,))) * size**-0.5
            out_ref[:, own] = turn(d_query, cosine, -sine).astype(b16)
            d_key += dot(d_scores, query, ((0,), (0,)))
            d_value += dot(probs.astype(b16), d_att, ((0,), (0,)))
        at = heads * size + kv * size
        out_ref[:, at : at + size] = turn(d_key, cosine, -sine).astype(b16)
        at += kv_heads * size
        out_ref[:, at : at + size] = d_value.astype(b16)


def one_block(body, outs, *args):
    return pl.pallas_call(
        body,
        out_shape=outs,
        in_specs=[pl.BlockSpec(memory_space=pltpu.VMEM)] * len(args),
        out_specs=jax.tree.map(lambda _: pl.BlockSpec(memory_space=pltpu.VMEM), outs),
        compiler_params=pltpu.CompilerParams(vmem_limit_bytes=40 << 20),
        cost_estimate=pl.CostEstimate(flops=1000, bytes_accessed=1000, transcendentals=0),
    )(*args)


def dot(lhs, rhs, dims):
    return lax.dot_general(lhs, rhs, (dims, ((), ())), preferred_element_type=f32)


def swap(piece, axis):
    return lax.ppermute(piece, axis, [(0, 1), (1, 0)])


def hop(piece, step, n):
    return lax.ppermute(piece, "fsdp", [(d, d ^ step) for d in range(n)])


def gather_rows(own, n, checks=()):
    have, near = [own], hop(own, 1, n)
    bit = n // 2
    while bit > 1:
        new = [hop(piece, bit, n) for piece in have]
        if len(have) == 1:
            new = [after(new[0], near)]
        have = have + new
        bit //= 2
    even = jnp.concatenate(have)
    odd = jnp.concatenate([near] + [hop(piece, 1, n) for piece in have[1:]])
    return [jnp.concatenate([part, swap(part, "tp")]) for part in (even, odd)], have[1]


def after(value, *others):
    return lax.optimization_barrier((value, *others))[0]


def scatter_blocks(blocks, bit, n, serial=False, gates=None):
    marks = []
    while bit < n:
        keep = len(blocks) // 2
        marks.append(blocks[-1])
        came = [None] * keep
        order = sorted(range(keep), key=lambda k: keys_of(n)[k], reverse=True)
        for at, k in enumerate(order):
            piece = blocks[keep + k].astype(b16)
            if serial and bit == 1 and at:
                piece = after(piece, came[order[at - 1]], *gates.get(at, ()))
            came[k] = hop(piece, bit, n)
            if serial and bit == 1 and at == 1:
                marks[0] = came[k]
        blocks = [block + piece.astype(f32) for block, piece in zip(blocks, came)]
        bit *= 2
    return blocks[0], marks


def scatter_rows(product, sources, n):
    half = sources[0].shape[0] // 2
    rows = 2 * half // n
    take = lambda k: product(sources[k % 2][k // 2 * half : (k // 2 + 1) * half])
    far = [swap(take(k).astype(b16), "tp") for k in (3, 2)]
    odd = take(1) + far[0].astype(f32)
    even = take(0) + far[1].astype(f32)
    blocks = [part[k * rows : (k + 1) * rows] for part in (even, odd) for k in range(n // 2)]
    own, marks = scatter_blocks(blocks, 1, n)
    return own, [odd] + marks[1:]


def gather_group(own):
    across = swap(own, "ctx")
    beside = swap(jnp.concatenate([own, across]), "tp")
    rows = own.shape[0]
    return jnp.concatenate([own, beside[:rows], across, beside[rows:]])


def scatter_group(part):
    rows = part.shape[0] // 4
    b0, b1, b2, b3 = [part[k * rows : (k + 1) * rows] for k in range(4)]
    got = swap(jnp.concatenate([b1, b3]), "tp")
    return b0 + got[:rows] + swap((b2 + got[rows:]).astype(b16), "ctx").astype(f32)


def keys_of(n):
    order, bit = [0], n // 2
    while bit:
        order = order + [k ^ bit for k in order]
        bit //= 2
    return order


def tile_window(units, n):
    spans = [-(-(d + 1) * units // 128) - d * units // 128 for d in range(n)]
    return 128 * max(spans)


def natural(own, other, index, axis):
    first = jnp.where(index == 0, own, other)
    second = jnp.where(index == 0, other, own)
    return jnp.concatenate([first, second], axis=axis)


def local(
    n,
    tokens,
    cotangent,
    lengths,
    positions,
    query_weight,
    key_weight,
    value_weight,
    output_weight,
    gate_weight,
    up_weight,
    down_weight,
    gain_attn_in,
    gain_attn_out,
    gain_ffn_in,
    gain_ffn_out,
):
    me = lax.axis_index("fsdp")
    ctx = lax.axis_index("ctx")
    tp = lax.axis_index("tp")
    tok_rows, width = tokens.shape
    rows = tok_rows // 2
    head_size = HEAD_DIM
    d_rows = query_weight.shape[0]
    d_half = d_rows // 2
    q_cols = query_weight.shape[1] // 2
    k_cols = key_weight.shape[1] // 2
    q_local = q_cols // head_size
    kv_local = k_cols // head_size
    ff_local = gate_weight.shape[1]
    ff_own = ff_local // n

    starts = [
        c * tok_rows + t * rows for c in (ctx, 1 - ctx) for t in (tp, 1 - tp)
    ]
    packed = jnp.concatenate(
        [lax.dynamic_slice_in_dim(positions[0], start, rows) for start in starts]
    )
    segment, inner = placement_of(lengths[0], packed)
    angles = angles_of(inner, head_size)

    mine = lax.dynamic_slice_in_dim(tokens, tp * rows, rows)
    across = swap(mine, "ctx")
    beside = swap(across, "tp")
    seq_group = jnp.concatenate([tokens, across, beside])
    row_ids = jnp.arange(rows, dtype=jnp.int32)
    seq_ids = jnp.concatenate(
        [ctx * tok_rows + jnp.arange(tok_rows, dtype=jnp.int32), starts[2] + row_ids, starts[3] + row_ids]
    )
    pick = (packed[:, None] == seq_ids[None, :]).astype(b16)
    slot_in = dot(pick, seq_group, ((1,), (0,)))
    resid_in = slot_in[:rows]

    gain_row = jnp.concatenate([gain_attn_in, gain_attn_out, gain_ffn_in, gain_ffn_out])
    heads_cols = q_cols + 2 * k_cols
    gain_rows = -(-4 * d_rows // heads_cols)
    heads_own = jnp.concatenate(
        [
            lax.dynamic_slice_in_dim(query_weight, ctx * q_cols, q_cols, 1),
            lax.dynamic_slice_in_dim(key_weight, ctx * k_cols, k_cols, 1),
            lax.dynamic_slice_in_dim(value_weight, ctx * k_cols, k_cols, 1),
        ],
        axis=1,
    )
    heads_own = jnp.concatenate(
        [heads_own, jnp.pad(gain_row, (0, 16 * heads_cols - 4 * d_rows)).reshape(16, heads_cols)]
    )
    have = [(0, heads_own)]
    bit = n // 2
    while bit:
        have = have + [(k ^ bit, hop(piece, bit, n)) for k, piece in have]
        bit //= 2
    out_own = lax.dynamic_slice_in_dim(output_weight, ctx * q_cols, q_cols, 0).T
    out_weight = lax.all_gather(out_own, "fsdp", axis=0, tiled=True)
    qkv_weight = jnp.zeros((n, d_rows, heads_cols), b16)
    gains = jnp.zeros((n, gain_rows, heads_cols), b16)
    for k, piece in have:
        put = lambda whole, part: lax.dynamic_update_slice_in_dim(whole, part[None], me ^ k, 0)
        qkv_weight = put(qkv_weight, piece[:d_rows])
        gains = put(gains, piece[d_rows : d_rows + gain_rows])
    qkv_weight = qkv_weight.reshape(width, heads_cols)
    gains = gains.reshape(n, gain_rows * heads_cols)[:, : 4 * d_rows]
    gains = gains.reshape(n, 4, d_rows).transpose(1, 0, 2).reshape(4, width).astype(f32)

    window = tile_window(ff_own, n)
    first = lambda device: (device * ff_own) & -128
    unit = first(me) + jnp.arange(window, dtype=jnp.int32)
    valid = ((unit >= me * ff_own) & (unit < (me + 1) * ff_own))[None]

    def to_units(weights):
        halves = [lax.dynamic_slice_in_dim(weight, ctx * d_half, d_half) for weight in weights]
        own = jnp.stack(
            [
                jnp.concatenate([half[:, first(d) : first(d) + window] for half in halves], axis=1)
                for d in range(n)
            ]
        )
        return lax.all_to_all(own, "fsdp", 0, 0, tiled=True)

    def both_halves(half, other):
        whole = jnp.zeros((n, 2, *half.shape[1:]), b16)
        whole = lax.dynamic_update_slice_in_dim(whole, half[:, None], ctx, 1)
        whole = lax.dynamic_update_slice_in_dim(whole, other[:, None], 1 - ctx, 1)
        return whole.reshape(width, half.shape[2])

    far_piece = have[n // 2 - 1][1]
    gu_half = to_units([after(weight, far_piece) for weight in (gate_weight, up_weight)])

    normed_attn = rms_scale(slot_in, gains[0]).astype(b16)
    qkv = dot(normed_attn, qkv_weight, ((1,), (0,)))
    all_rows = 2 * tok_rows
    cosine, sine = jnp.cos(angles), jnp.sin(angles)
    places = jnp.stack([segment, inner])
    held = lambda cols: jax.ShapeDtypeStruct((all_rows, cols), b16)
    attended, queries, keys, values = one_block(
        functools.partial(attend_body, q_local, kv_local),
        [held(q_cols), held(q_cols), held(k_cols), held(k_cols)],
        qkv,
        cosine,
        sine,
        places.T,
        places,
    )
    attn_out = scatter_group(dot(attended, out_weight, ((1,), (1,))))
    middle = resid_in + rms_scale(attn_out, gains[1])

    normed_own = rms_scale(middle, gains[2]).astype(b16)
    gu_other = swap(after(gu_half, attn_out), "ctx")
    normed_ffn, mark = gather_rows(normed_own, n)
    down_half = to_units([after(down_weight.T, mark)])
    down_other = swap(after(down_half, gu_other), "ctx")
    gu_full = both_halves(gu_half, gu_other)
    down_full = both_halves(down_half, down_other)
    gates_and_ups = [dot(part, gu_full, ((1,), (0,))) for part in normed_ffn]
    acts = [(part[:, :window], part[:, window:]) for part in gates_and_ups]
    hidden = [jnp.where(valid, glu_apply(*pair), 0.0).astype(b16) for pair in acts]
    ffn_out, _ = scatter_rows(lambda part: dot(part, down_full, ((1,), (1,))), hidden, n)
    block_own = (middle + rms_scale(ffn_out, gains[3])).astype(b16)
    block_out = natural(block_own, swap(block_own, "tp"), tp, 0)

    d_out = lax.dynamic_slice_in_dim(cotangent, tp * rows, rows).astype(f32)
    d_ffn_raw, gain_four_term = norm_back(ffn_out, gains[3], d_out)
    d_ffn_out, _ = gather_rows(d_ffn_raw.astype(b16), n)
    d_pairs = [
        jax.vjp(glu_apply, *pair)[1](dot(part, down_full, ((1,), (0,))))
        for pair, part in zip(acts, d_ffn_out)
    ]
    d_pairs = [[jnp.where(valid, part, 0.0).astype(b16) for part in pair] for pair in d_pairs]
    d_normed_ffn, marks = scatter_rows(
        lambda part: dot(part, gu_full, ((1,), (1,))),
        [jnp.concatenate(pair, axis=1) for pair in d_pairs],
        n,
    )

    def halves(terms):
        terms = terms.reshape(n, 2, d_half, window)
        send = lax.dynamic_index_in_dim(terms, 1 - ctx, 1, keepdims=False).astype(b16)
        return send, lax.dynamic_index_in_dim(terms, ctx, 1, keepdims=False)

    hidden, d_ffn_out, normed_ffn = [
        jnp.concatenate([after(part, marks[0]) for part in parts])
        for parts in (hidden, d_ffn_out, normed_ffn)
    ]
    d_gate, d_up = [jnp.concatenate(parts) for parts in zip(*d_pairs)]
    down_send, down_keep = halves(dot(d_ffn_out, hidden, ((0,), (0,))))
    late_normed = after(normed_ffn, marks[-1], down_send)
    gate_send, gate_keep = halves(dot(late_normed, d_gate, ((0,), (0,))))
    up_send, up_keep = halves(dot(after(late_normed, gate_send), d_up, ((0,), (0,))))
    down_got, gate_got = swap(down_send, "ctx"), swap(gate_send, "ctx")

    def to_owners(keeps, gots, gate):
        gots = [after(got, gate) for got in gots]
        low = [(keep + got.astype(f32)).astype(b16) for keep, got in zip(keeps, gots)]
        return lax.all_to_all(jnp.concatenate(low, axis=2), "fsdp", 0, 0, tiled=True)

    def columns_joined(whole):
        period = 128 // math.gcd(ff_own, 128)
        tiles = period * ff_own // 128
        parts = whole.reshape(n // period, period, *whole.shape[1:]).astype(f32)
        runs = []
        for tile in range(tiles):
            holds = [
                d
                for d in range(period)
                if d * ff_own < (tile + 1) * 128 and (d + 1) * ff_own > tile * 128
            ]
            if runs and runs[-1][0] == holds and len(holds) == 1:
                runs[-1][2] = tile + 1
            else:
                runs.append([holds, tile, tile + 1])
        pieces = [
            sum(parts[:, d, ..., a * 128 - first(d) : b * 128 - first(d)] for d in holds)
            for holds, a, b in runs
        ]
        joined = jnp.concatenate(pieces, axis=-1)
        return joined.transpose(1, 0, 2).reshape(whole.shape[1], ff_local)

    d_normed_ffn = after(d_normed_ffn, down_got, gate_send, up_send)
    d_middle_part, gain_three_term = norm_back(middle, gains[2], d_normed_ffn)
    d_middle = d_out + d_middle_part
    d_attn_raw, gain_two_term = norm_back(attn_out, gains[1], d_middle)
    d_attn_out = gather_group(d_attn_raw.astype(b16))
    up_got = swap(after(up_send, d_attn_out), "ctx")
    down_rows = to_owners([down_keep], [down_got], d_normed_ffn)
    d_attended = dot(d_attn_out, out_weight, ((1,), (0,))).astype(b16)
    d_qkv = one_block(
        functools.partial(attend_back_body, q_local, kv_local),
        held(q_cols + 2 * k_cols),
        d_attended,
        queries,
        keys,
        values,
        cosine,
        sine,
        places.T,
        places,
    )
    d_normed_part = dot(d_qkv, qkv_weight, ((1,), (1,)))
    d_normed_attn = scatter_group(d_normed_part)
    resid_part, gain_one_term = norm_back(resid_in, gains[0], d_normed_attn)
    slot_grad = gather_group((d_middle + resid_part).astype(b16))
    unpick = (
        (ctx * tok_rows + jnp.arange(tok_rows, dtype=jnp.int32))[:, None] == packed[None, :]
    ).astype(b16)
    tokens_grad = dot(unpick, slot_grad, ((1,), (0,))).astype(b16)

    down_weight_grad = columns_joined(down_rows).T
    attn_terms = [
        dot(normed_attn, d_qkv, ((0,), (0,))).reshape(n, d_rows, -1),
        dot(d_attn_out, attended, ((0,), (0,))).reshape(n, d_rows, -1),
    ]
    attn_rows, marks = scatter_blocks(
        [
            jnp.concatenate(
                [lax.dynamic_index_in_dim(terms, me ^ k, 0, keepdims=False) for terms in attn_terms],
                axis=1,
            )
            for k in keys_of(n)
        ],
        1,
        n,
        serial=True,
        gates={1: [down_rows], 2: [down_weight_grad]},
    )
    gu_rows = after(to_owners([gate_keep, up_keep], [gate_got, up_got], marks[0]), attn_rows)
    gate_rows, up_rows = gu_rows[..., :window], gu_rows[..., window:]
    gate_weight_grad = columns_joined(gate_rows)
    up_weight_grad = columns_joined(up_rows)
    attn_rows = attn_rows.reshape(2, d_half, -1)
    attn_own = lax.dynamic_index_in_dim(attn_rows, ctx, 0, keepdims=False)
    attn_other = swap(
        lax.dynamic_index_in_dim(attn_rows, 1 - ctx, 0, keepdims=False).astype(b16), "ctx"
    )
    edges = [0, q_cols, q_cols + k_cols, q_cols + 2 * k_cols, 2 * q_cols + 2 * k_cols]
    attn_grads = [
        natural(attn_own[:, a:b].astype(f32), attn_other[:, a:b].astype(f32), ctx, 1)
        for a, b in zip(edges[:-1], edges[1:])
    ]

    gain_terms = jnp.stack([gain_one_term, gain_two_term, gain_three_term, gain_four_term])
    gain_terms = gain_terms + swap(gain_terms, "tp")
    gain_terms = gain_terms.reshape(4, n, 2, d_half).transpose(1, 2, 0, 3)
    gain_terms = lax.dynamic_index_in_dim(gain_terms, ctx, 1, keepdims=False) + swap(
        lax.dynamic_index_in_dim(gain_terms, 1 - ctx, 1, keepdims=False), "ctx"
    )
    gain_rows = jnp.stack(
        [lax.dynamic_index_in_dim(gain_terms, me ^ k, 0, keepdims=False) for k in keys_of(n)]
    )
    gain_rows = after(gain_rows, attn_other)
    bit = 1
    while bit < n:
        keep = gain_rows.shape[0] // 2
        gain_rows = gain_rows[:keep] + hop(gain_rows[keep:], bit, n)
        bit *= 2
    gain_rows = gain_rows[0]
    return (
        block_out,
        tokens_grad,
        attn_grads[0],
        attn_grads[1],
        attn_grads[2],
        attn_grads[3].T,
        gate_weight_grad,
        up_weight_grad,
        down_weight_grad,
        gain_rows[0],
        gain_rows[1],
        gain_rows[2],
        gain_rows[3],
    )


def solution(mesh):
    in_specs = (
        P(("fsdp", "ctx"), None),
        P(("fsdp", "ctx"), None),
        P("fsdp", None),
        P("fsdp", None),
        P("fsdp", "tp"),
        P("fsdp", "tp"),
        P("fsdp", "tp"),
        P("tp", "fsdp"),
        P("fsdp", "tp"),
        P("fsdp", "tp"),
        P("tp", "fsdp"),
        P("fsdp"),
        P("fsdp"),
        P("fsdp"),
        P("fsdp"),
    )
    out_specs = (
        P(("fsdp", "ctx"), None),
        P(("fsdp", "ctx"), None),
        P(("fsdp", "ctx"), "tp"),
        P(("fsdp", "ctx"), "tp"),
        P(("fsdp", "ctx"), "tp"),
        P("tp", ("fsdp", "ctx")),
        P(("fsdp", "ctx"), "tp"),
        P(("fsdp", "ctx"), "tp"),
        P("tp", ("fsdp", "ctx")),
        P(("fsdp", "ctx")),
        P(("fsdp", "ctx")),
        P(("fsdp", "ctx")),
        P(("fsdp", "ctx")),
    )
    step = functools.partial(local, mesh.shape["fsdp"])
    return jax.shard_map(step, mesh=mesh, in_specs=in_specs, out_specs=out_specs, check_vma=False)
```

```python
import functools
import math

import jax
import jax.numpy as jnp
from jax import lax
from jax.experimental import pallas as pl
from jax.experimental.pallas import tpu as pltpu
from jax.sharding import PartitionSpec as P

HEAD_DIM = 256

eps_norm = 1e-06
soft_cap = 50.0
f32 = jnp.float32
b16 = jnp.bfloat16


def rms_scale(field, gain_vec):
    factor = lax.rsqrt(jnp.mean(field * field, axis=-1, keepdims=True) + eps_norm)
    return field * factor * (1.0 + gain_vec)


def gelu_tanh(value_in):
    return (
        0.5
        * value_in
        * (
            1.0
            + jnp.tanh(0.7978845608028654 * (value_in + 0.044715 * value_in * value_in * value_in))
        )
    )


def glu_apply(gate_act, up_act):
    return gelu_tanh(gate_act) * up_act


def norm_back(field, gain_vec, cot_in):
    pullback = jax.vjp(rms_scale, field, gain_vec)[1]
    return pullback(cot_in)


def placement_of(doc_lengths, packed):
    doc_ends = jnp.cumsum(doc_lengths)
    after_end = packed[:, None] >= doc_ends[None, :]
    segment = jnp.sum(after_end.astype(jnp.int32), axis=1)
    inner = packed - jnp.sum(jnp.where(after_end, doc_lengths[None, :], 0), axis=1)
    return (segment, inner)


def angles_of(inner, head_size):
    half_size = head_size // 2
    freq = jnp.power(10000.0, -jnp.arange(half_size, dtype=f32) * (2.0 / head_size))
    return inner.astype(f32)[:, None] * freq[None, :]


def turn(field, cosine, sine):
    half = field.shape[1] // 2
    first, second = field[:, :half], field[:, half:]
    return jnp.concatenate(
        [first * cosine - second * sine, second * cosine + first * sine], axis=1
    )


def softmax_of(query, key, allowed):
    ratio = jnp.tanh(dot(query, key, ((1,), (1,))) / soft_cap)
    masked = jnp.where(allowed, soft_cap * ratio, -1e30)
    terms = jnp.exp(masked - jnp.max(masked, axis=1, keepdims=True))
    return ratio, terms / jnp.sum(terms, axis=1, keepdims=True)


def allowed_of(row_ref, col_ref):
    segment, inner = row_ref[:, 0:1], row_ref[:, 1:2]
    return (segment == col_ref[0:1, :]) & (col_ref[1:2, :] <= inner)


def attend_body(heads, kv_heads, qkv_ref, cos_ref, sin_ref, row_ref, col_ref, *out_refs):
    attended_ref, query_ref, key_ref, value_ref = out_refs
    size = HEAD_DIM
    allowed = allowed_of(row_ref, col_ref)
    cosine, sine = cos_ref[...], sin_ref[...]
    for kv in range(kv_heads):
        own = slice(kv * size, (kv + 1) * size)
        at = heads * size + kv * size
        key = turn(qkv_ref[:, at : at + size], cosine, sine).astype(b16)
        at += kv_heads * size
        value = qkv_ref[:, at : at + size].astype(b16)
        key_ref[:, own] = key
        value_ref[:, own] = value
        for head in range(kv * heads // kv_heads, (kv + 1) * heads // kv_heads):
            own = slice(head * size, (head + 1) * size)
            query = (turn(qkv_ref[:, own], cosine, sine) * size**-0.5).astype(b16)
            query_ref[:, own] = query
            _, probs = softmax_of(query, key, allowed)
            attended_ref[:, own] = dot(probs.astype(b16), value, ((1,), (0,))).astype(b16)


def attend_back_body(heads, kv_heads, d_att_ref, query_ref, key_ref, value_ref, cos_ref, sin_ref, row_ref, col_ref, out_ref):
    size = HEAD_DIM
    allowed = allowed_of(row_ref, col_ref)
    cosine, sine = cos_ref[...], sin_ref[...]
    for kv in range(kv_heads):
        own = slice(kv * size, (kv + 1) * size)
        key, value = key_ref[:, own], value_ref[:, own]
        d_key = d_value = 0.0
        for head in range(kv * heads // kv_heads, (kv + 1) * heads // kv_heads):
            own = slice(head * size, (head + 1) * size)
            query, d_att = query_ref[:, own], d_att_ref[:, own]
            ratio, probs = softmax_of(query, key, allowed)
            d_probs = dot(d_att, value, ((1,), (1,)))
            d_soft = probs * (d_probs - jnp.sum(probs * d_probs, axis=1, keepdims=True))
            d_scores = (d_soft * (1.0 - ratio * ratio)).astype(b16)
            d_query = dot(d_scores, key, ((1,), (0,))) * size**-0.5
            out_ref[:, own] = turn(d_query, cosine, -sine).astype(b16)
            d_key += dot(d_scores, query, ((0,), (0,)))
            d_value += dot(probs.astype(b16), d_att, ((0,), (0,)))
        at = heads * size + kv * size
        out_ref[:, at : at + size] = turn(d_key, cosine, -sine).astype(b16)
        at += kv_heads * size
        out_ref[:, at : at + size] = d_value.astype(b16)


def one_block(body, outs, *args):
    return pl.pallas_call(
        body,
        out_shape=outs,
        in_specs=[pl.BlockSpec(memory_space=pltpu.VMEM)] * len(args),
        out_specs=jax.tree.map(lambda _: pl.BlockSpec(memory_space=pltpu.VMEM), outs),
        compiler_params=pltpu.CompilerParams(vmem_limit_bytes=40 << 20),
        cost_estimate=pl.CostEstimate(flops=1000, bytes_accessed=1000, transcendentals=0),
    )(*args)


def dot(lhs, rhs, dims):
    return lax.dot_general(lhs, rhs, (dims, ((), ())), preferred_element_type=f32)


def swap(piece, axis):
    return lax.ppermute(piece, axis, [(0, 1), (1, 0)])


def hop(piece, step, n):
    return lax.ppermute(piece, "fsdp", [(d, d ^ step) for d in range(n)])


def gather_rows(own, n, checks=()):
    have, near = [own], hop(own, 1, n)
    bit = n // 2
    while bit > 1:
        new = [hop(piece, bit, n) for piece in have]
        if len(have) == 1:
            new = [after(new[0], near)]
        have = have + new
        bit //= 2
    even = jnp.concatenate(have)
    odd = jnp.concatenate([near] + [hop(piece, 1, n) for piece in have[1:]])
    return [jnp.concatenate([part, swap(part, "tp")]) for part in (even, odd)], have[1]


def after(value, *others):
    return lax.optimization_barrier((value, *others))[0]


def scatter_blocks(blocks, bit, n, serial=False, gates=None):
    marks = []
    while bit < n:
        keep = len(blocks) // 2
        marks.append(blocks[-1])
        came = [None] * keep
        order = sorted(range(keep), key=lambda k: keys_of(n)[k], reverse=True)
        for at, k in enumerate(order):
            piece = blocks[keep + k].astype(b16)
            if serial and bit == 1 and at:
                piece = after(piece, came[order[at - 1]], *gates.get(at, ()))
            came[k] = hop(piece, bit, n)
            if serial and bit == 1 and at == 1:
                marks[0] = came[k]
        blocks = [block + piece.astype(f32) for block, piece in zip(blocks, came)]
        bit *= 2
    return blocks[0], marks


def scatter_rows(product, sources, n):
    half = sources[0].shape[0] // 2
    rows = 2 * half // n
    take = lambda k: product(sources[k % 2][k // 2 * half : (k // 2 + 1) * half])
    far = [swap(take(k).astype(b16), "tp") for k in (3, 2)]
    odd = take(1) + far[0].astype(f32)
    even = take(0) + far[1].astype(f32)
    blocks = [part[k * rows : (k + 1) * rows] for part in (even, odd) for k in range(n // 2)]
    own, marks = scatter_blocks(blocks, 1, n)
    return own, [odd] + marks[1:]


def gather_group(own):
    across = swap(own, "ctx")
    beside = swap(jnp.concatenate([own, across]), "tp")
    rows = own.shape[0]
    return jnp.concatenate([own, beside[:rows], across, beside[rows:]])


def scatter_group(part):
    rows = part.shape[0] // 4
    b0, b1, b2, b3 = [part[k * rows : (k + 1) * rows] for k in range(4)]
    got = swap(jnp.concatenate([b1, b3]), "tp")
    return b0 + got[:rows] + swap((b2 + got[rows:]).astype(b16), "ctx").astype(f32)


def keys_of(n):
    order, bit = [0], n // 2
    while bit:
        order = order + [k ^ bit for k in order]
        bit //= 2
    return order


def tile_window(units, n):
    spans = [-(-(d + 1) * units // 128) - d * units // 128 for d in range(n)]
    return 128 * max(spans)


def natural(own, other, index, axis):
    first = jnp.where(index == 0, own, other)
    second = jnp.where(index == 0, other, own)
    return jnp.concatenate([first, second], axis=axis)


def local(
    n,
    tokens,
    cotangent,
    lengths,
    positions,
    query_weight,
    key_weight,
    value_weight,
    output_weight,
    gate_weight,
    up_weight,
    down_weight,
    gain_attn_in,
    gain_attn_out,
    gain_ffn_in,
    gain_ffn_out,
):
    me = lax.axis_index("fsdp")
    ctx = lax.axis_index("ctx")
    tp = lax.axis_index("tp")
    tok_rows, width = tokens.shape
    rows = tok_rows // 2
    head_size = HEAD_DIM
    d_rows = query_weight.shape[0]
    d_half = d_rows // 2
    q_cols = query_weight.shape[1] // 2
    k_cols = key_weight.shape[1] // 2
    q_local = q_cols // head_size
    kv_local = k_cols // head_size
    ff_local = gate_weight.shape[1]
    ff_own = ff_local // n

    starts = [
        c * tok_rows + t * rows for c in (ctx, 1 - ctx) for t in (tp, 1 - tp)
    ]
    packed = jnp.concatenate(
        [lax.dynamic_slice_in_dim(positions[0], start, rows) for start in starts]
    )
    segment, inner = placement_of(lengths[0], packed)
    angles = angles_of(inner, head_size)

    mine = lax.dynamic_slice_in_dim(tokens, tp * rows, rows)
    across = swap(mine, "ctx")
    beside = swap(across, "tp")
    seq_group = jnp.concatenate([tokens, across, beside])
    row_ids = jnp.arange(rows, dtype=jnp.int32)
    seq_ids = jnp.concatenate(
        [ctx * tok_rows + jnp.arange(tok_rows, dtype=jnp.int32), starts[2] + row_ids, starts[3] + row_ids]
    )
    pick = (packed[:, None] == seq_ids[None, :]).astype(b16)
    slot_in = dot(pick, seq_group, ((1,), (0,)))
    resid_in = slot_in[:rows]

    gain_row = jnp.concatenate([gain_attn_in, gain_attn_out, gain_ffn_in, gain_ffn_out])
    heads_cols = q_cols + 2 * k_cols
    gain_rows = -(-4 * d_rows // heads_cols)
    heads_own = jnp.concatenate(
        [
            lax.dynamic_slice_in_dim(query_weight, ctx * q_cols, q_cols, 1),
            lax.dynamic_slice_in_dim(key_weight, ctx * k_cols, k_cols, 1),
            lax.dynamic_slice_in_dim(value_weight, ctx * k_cols, k_cols, 1),
        ],
        axis=1,
    )
    heads_own = jnp.concatenate(
        [heads_own, jnp.pad(gain_row, (0, 16 * heads_cols - 4 * d_rows)).reshape(16, heads_cols)]
    )
    have = [(0, heads_own)]
    bit = n // 2
    while bit:
        have = have + [(k ^ bit, hop(piece, bit, n)) for k, piece in have]
        bit //= 2
    out_own = lax.dynamic_slice_in_dim(output_weight, ctx * q_cols, q_cols, 0).T
    out_weight = lax.all_gather(out_own, "fsdp", axis=0, tiled=True)
    qkv_weight = jnp.zeros((n, d_rows, heads_cols), b16)
    gains = jnp.zeros((n, gain_rows, heads_cols), b16)
    for k, piece in have:
        put = lambda whole, part: lax.dynamic_update_slice_in_dim(whole, part[None], me ^ k, 0)
        qkv_weight = put(qkv_weight, piece[:d_rows])
        gains = put(gains, piece[d_rows : d_rows + gain_rows])
    qkv_weight = qkv_weight.reshape(width, heads_cols)
    gains = gains.reshape(n, gain_rows * heads_cols)[:, : 4 * d_rows]
    gains = gains.reshape(n, 4, d_rows).transpose(1, 0, 2).reshape(4, width).astype(f32)

    window = tile_window(ff_own, n)
    first = lambda device: (device * ff_own) & -128
    unit = first(me) + jnp.arange(window, dtype=jnp.int32)
    valid = ((unit >= me * ff_own) & (unit < (me + 1) * ff_own))[None]

    def to_units(weights):
        halves = [lax.dynamic_slice_in_dim(weight, ctx * d_half, d_half) for weight in weights]
        own = jnp.stack(
            [
                jnp.concatenate([half[:, first(d) : first(d) + window] for half in halves], axis=1)
                for d in range(n)
            ]
        )
        return lax.all_to_all(own, "fsdp", 0, 0, tiled=True)

    def both_halves(half, other):
        whole = jnp.zeros((n, 2, *half.shape[1:]), b16)
        whole = lax.dynamic_update_slice_in_dim(whole, half[:, None], ctx, 1)
        whole = lax.dynamic_update_slice_in_dim(whole, other[:, None], 1 - ctx, 1)
        return whole.reshape(width, half.shape[2])

    far_piece = have[n // 2 - 1][1]
    gu_half = to_units([after(weight, far_piece) for weight in (gate_weight, up_weight)])

    normed_attn = rms_scale(slot_in, gains[0]).astype(b16)
    qkv = dot(normed_attn, qkv_weight, ((1,), (0,)))
    all_rows = 2 * tok_rows
    cosine, sine = jnp.cos(angles), jnp.sin(angles)
    places = jnp.stack([segment, inner])
    held = lambda cols: jax.ShapeDtypeStruct((all_rows, cols), b16)
    attended, queries, keys, values = one_block(
        functools.partial(attend_body, q_local, kv_local),
        [held(q_cols), held(q_cols), held(k_cols), held(k_cols)],
        qkv,
        cosine,
        sine,
        places.T,
        places,
    )
    attn_out = scatter_group(dot(attended, out_weight, ((1,), (1,))))
    middle = resid_in + rms_scale(attn_out, gains[1])

    normed_own = rms_scale(middle, gains[2]).astype(b16)
    gu_other = swap(after(gu_half, attn_out), "ctx")
    normed_ffn, mark = gather_rows(normed_own, n)
    down_half = to_units([after(down_weight.T, mark)])
    down_other = swap(after(down_half, gu_other), "ctx")
    gu_full = both_halves(gu_half, gu_other)
    down_full = both_halves(down_half, down_other)
    gates_and_ups = [dot(part, gu_full, ((1,), (0,))) for part in normed_ffn]
    acts = [(part[:, :window], part[:, window:]) for part in gates_and_ups]
    hidden = [jnp.where(valid, glu_apply(*pair), 0.0).astype(b16) for pair in acts]
    ffn_out, _ = scatter_rows(lambda part: dot(part, down_full, ((1,), (1,))), hidden, n)
    block_own = (middle + rms_scale(ffn_out, gains[3])).astype(b16)
    block_out = natural(block_own, swap(block_own, "tp"), tp, 0)

    d_out = lax.dynamic_slice_in_dim(cotangent, tp * rows, rows).astype(f32)
    d_ffn_raw, gain_four_term = norm_back(ffn_out, gains[3], d_out)
    d_ffn_out, _ = gather_rows(d_ffn_raw.astype(b16), n)
    d_pairs = [
        jax.vjp(glu_apply, *pair)[1](dot(part, down_full, ((1,), (0,))))
        for pair, part in zip(acts, d_ffn_out)
    ]
    d_pairs = [[jnp.where(valid, part, 0.0).astype(b16) for part in pair] for pair in d_pairs]
    d_normed_ffn, marks = scatter_rows(
        lambda part: dot(part, gu_full, ((1,), (1,))),
        [jnp.concatenate(pair, axis=1) for pair in d_pairs],
        n,
    )

    def halves(terms):
        terms = terms.reshape(n, 2, d_half, window)
        send = lax.dynamic_index_in_dim(terms, 1 - ctx, 1, keepdims=False).astype(b16)
        return send, lax.dynamic_index_in_dim(terms, ctx, 1, keepdims=False)

    hidden, d_ffn_out, normed_ffn = [
        jnp.concatenate([after(part, marks[0]) for part in parts])
        for parts in (hidden, d_ffn_out, normed_ffn)
    ]
    d_gate, d_up = [jnp.concatenate(parts) for parts in zip(*d_pairs)]
    down_send, down_keep = halves(dot(d_ffn_out, hidden, ((0,), (0,))))
    late_normed = after(normed_ffn, marks[-1], down_send)
    gate_send, gate_keep = halves(dot(late_normed, d_gate, ((0,), (0,))))
    up_send, up_keep = halves(dot(after(late_normed, gate_send), d_up, ((0,), (0,))))
    down_got, gate_got = swap(down_send, "ctx"), swap(gate_send, "ctx")

    def to_owners(keeps, gots, gate):
        gots = [after(got, gate) for got in gots]
        low = [(keep + got.astype(f32)).astype(b16) for keep, got in zip(keeps, gots)]
        return lax.all_to_all(jnp.concatenate(low, axis=2), "fsdp", 0, 0, tiled=True)

    def columns_joined(whole):
        period = 128 // math.gcd(ff_own, 128)
        tiles = period * ff_own // 128
        parts = whole.reshape(n // period, period, *whole.shape[1:]).astype(f32)
        runs = []
        for tile in range(tiles):
            holds = [
                d
                for d in range(period)
                if d * ff_own < (tile + 1) * 128 and (d + 1) * ff_own > tile * 128
            ]
            if runs and runs[-1][0] == holds and len(holds) == 1:
                runs[-1][2] = tile + 1
            else:
                runs.append([holds, tile, tile + 1])
        pieces = [
            sum(parts[:, d, ..., a * 128 - first(d) : b * 128 - first(d)] for d in holds)
            for holds, a, b in runs
        ]
        joined = jnp.concatenate(pieces, axis=-1)
        return joined.transpose(1, 0, 2).reshape(whole.shape[1], ff_local)

    d_normed_ffn = after(d_normed_ffn, down_got, gate_send, up_send)
    d_middle_part, gain_three_term = norm_back(middle, gains[2], d_normed_ffn)
    d_middle = d_out + d_middle_part
    d_attn_raw, gain_two_term = norm_back(attn_out, gains[1], d_middle)
    d_attn_out = gather_group(d_attn_raw.astype(b16))
    up_got = swap(after(up_send, d_attn_out), "ctx")
    down_rows = to_owners([down_keep], [down_got], d_normed_ffn)
    d_attended = dot(d_attn_out, out_weight, ((1,), (0,))).astype(b16)
    d_qkv = one_block(
        functools.partial(attend_back_body, q_local, kv_local),
        held(q_cols + 2 * k_cols),
        d_attended,
        queries,
        keys,
        values,
        cosine,
        sine,
        places.T,
        places,
    )
    d_normed_part = dot(d_qkv, qkv_weight, ((1,), (1,)))
    d_normed_attn = scatter_group(d_normed_part)
    resid_part, gain_one_term = norm_back(resid_in, gains[0], d_normed_attn)
    slot_grad = gather_group((d_middle + resid_part).astype(b16))
    unpick = (
        (ctx * tok_rows + jnp.arange(tok_rows, dtype=jnp.int32))[:, None] == packed[None, :]
    ).astype(b16)
    tokens_grad = dot(unpick, slot_grad, ((1,), (0,))).astype(b16)

    down_weight_grad = columns_joined(down_rows).T
    attn_terms = [
        dot(normed_attn, d_qkv, ((0,), (0,))).reshape(n, d_rows, -1),
        dot(d_attn_out, attended, ((0,), (0,))).reshape(n, d_rows, -1),
    ]
    attn_rows, marks = scatter_blocks(
        [
            jnp.concatenate(
                [lax.dynamic_index_in_dim(terms, me ^ k, 0, keepdims=False) for terms in attn_terms],
                axis=1,
            )
            for k in keys_of(n)
        ],
        1,
        n,
        serial=True,
        gates={1: [down_rows], 2: [down_weight_grad]},
    )
    gu_rows = after(to_owners([gate_keep, up_keep], [gate_got, up_got], marks[0]), attn_rows)
    gate_rows, up_rows = gu_rows[..., :window], gu_rows[..., window:]
    gate_weight_grad = columns_joined(gate_rows)
    up_weight_grad = columns_joined(up_rows)
    attn_rows = attn_rows.reshape(2, d_half, -1)
    attn_own = lax.dynamic_index_in_dim(attn_rows, ctx, 0, keepdims=False)
    attn_other = swap(
        lax.dynamic_index_in_dim(attn_rows, 1 - ctx, 0, keepdims=False).astype(b16), "ctx"
    )
    attn_other = after(attn_other, gate_weight_grad, up_weight_grad)
    edges = [0, q_cols, q_cols + k_cols, q_cols + 2 * k_cols, 2 * q_cols + 2 * k_cols]
    attn_grads = [
        natural(attn_own[:, a:b].astype(f32), attn_other[:, a:b].astype(f32), ctx, 1)
        for a, b in zip(edges[:-1], edges[1:])
    ]

    gain_terms = jnp.stack([gain_one_term, gain_two_term, gain_three_term, gain_four_term])
    gain_terms = gain_terms + swap(gain_terms, "tp")
    gain_terms = gain_terms.reshape(4, n, 2, d_half).transpose(1, 2, 0, 3)
    gain_terms = lax.dynamic_index_in_dim(gain_terms, ctx, 1, keepdims=False) + swap(
        lax.dynamic_index_in_dim(gain_terms, 1 - ctx, 1, keepdims=False), "ctx"
    )
    gain_rows = jnp.stack(
        [lax.dynamic_index_in_dim(gain_terms, me ^ k, 0, keepdims=False) for k in keys_of(n)]
    )
    gain_rows = after(gain_rows, attn_rows)
    bit = 1
    while bit < n:
        keep = gain_rows.shape[0] // 2
        gain_rows = gain_rows[:keep] + hop(gain_rows[keep:], bit, n)
        bit *= 2
    gain_rows = gain_rows[0]
    return (
        block_out,
        tokens_grad,
        attn_grads[0],
        attn_grads[1],
        attn_grads[2],
        attn_grads[3].T,
        gate_weight_grad,
        up_weight_grad,
        down_weight_grad,
        gain_rows[0],
        gain_rows[1],
        gain_rows[2],
        gain_rows[3],
    )


def solution(mesh):
    in_specs = (
        P(("fsdp", "ctx"), None),
        P(("fsdp", "ctx"), None),
        P("fsdp", None),
        P("fsdp", None),
        P("fsdp", "tp"),
        P("fsdp", "tp"),
        P("fsdp", "tp"),
        P("tp", "fsdp"),
        P("fsdp", "tp"),
        P("fsdp", "tp"),
        P("tp", "fsdp"),
        P("fsdp"),
        P("fsdp"),
        P("fsdp"),
        P("fsdp"),
    )
    out_specs = (
        P(("fsdp", "ctx"), None),
        P(("fsdp", "ctx"), None),
        P(("fsdp", "ctx"), "tp"),
        P(("fsdp", "ctx"), "tp"),
        P(("fsdp", "ctx"), "tp"),
        P("tp", ("fsdp", "ctx")),
        P(("fsdp", "ctx"), "tp"),
        P(("fsdp", "ctx"), "tp"),
        P("tp", ("fsdp", "ctx")),
        P(("fsdp", "ctx")),
        P(("fsdp", "ctx")),
        P(("fsdp", "ctx")),
        P(("fsdp", "ctx")),
    )
    step = functools.partial(local, mesh.shape["fsdp"])
    return jax.shard_map(step, mesh=mesh, in_specs=in_specs, out_specs=out_specs, check_vma=False)
```

```python
import functools
import math

import jax
import jax.numpy as jnp
from jax import lax
from jax.experimental import pallas as pl
from jax.experimental.pallas import tpu as pltpu
from jax.sharding import PartitionSpec as P

HEAD_DIM = 256

eps_norm = 1e-06
soft_cap = 50.0
f32 = jnp.float32
b16 = jnp.bfloat16


def rms_scale(field, gain_vec):
    factor = lax.rsqrt(jnp.mean(field * field, axis=-1, keepdims=True) + eps_norm)
    return field * factor * (1.0 + gain_vec)


def gelu_tanh(value_in):
    return (
        0.5
        * value_in
        * (
            1.0
            + jnp.tanh(0.7978845608028654 * (value_in + 0.044715 * value_in * value_in * value_in))
        )
    )


def glu_apply(gate_act, up_act):
    return gelu_tanh(gate_act) * up_act


def norm_back(field, gain_vec, cot_in):
    pullback = jax.vjp(rms_scale, field, gain_vec)[1]
    return pullback(cot_in)


def placement_of(doc_lengths, packed):
    doc_ends = jnp.cumsum(doc_lengths)
    after_end = packed[:, None] >= doc_ends[None, :]
    segment = jnp.sum(after_end.astype(jnp.int32), axis=1)
    inner = packed - jnp.sum(jnp.where(after_end, doc_lengths[None, :], 0), axis=1)
    return (segment, inner)


def angles_of(inner, head_size):
    half_size = head_size // 2
    freq = jnp.power(10000.0, -jnp.arange(half_size, dtype=f32) * (2.0 / head_size))
    return inner.astype(f32)[:, None] * freq[None, :]


def turn(field, cosine, sine):
    half = field.shape[1] // 2
    first, second = field[:, :half], field[:, half:]
    return jnp.concatenate(
        [first * cosine - second * sine, second * cosine + first * sine], axis=1
    )


def softmax_of(query, key, allowed):
    ratio = jnp.tanh(dot(query, key, ((1,), (1,))) / soft_cap)
    masked = jnp.where(allowed, soft_cap * ratio, -1e30)
    terms = jnp.exp(masked - jnp.max(masked, axis=1, keepdims=True))
    return ratio, terms / jnp.sum(terms, axis=1, keepdims=True)


def allowed_of(row_ref, col_ref):
    segment, inner = row_ref[:, 0:1], row_ref[:, 1:2]
    return (segment == col_ref[0:1, :]) & (col_ref[1:2, :] <= inner)


def attend_body(heads, kv_heads, qkv_ref, cos_ref, sin_ref, row_ref, col_ref, *out_refs):
    attended_ref, query_ref, key_ref, value_ref = out_refs
    size = HEAD_DIM
    allowed = allowed_of(row_ref, col_ref)
    cosine, sine = cos_ref[...], sin_ref[...]
    for kv in range(kv_heads):
        own = slice(kv * size, (kv + 1) * size)
        at = heads * size + kv * size
        key = turn(qkv_ref[:, at : at + size], cosine, sine).astype(b16)
        at += kv_heads * size
        value = qkv_ref[:, at : at + size].astype(b16)
        key_ref[:, own] = key
        value_ref[:, own] = value
        for head in range(kv * heads // kv_heads, (kv + 1) * heads // kv_heads):
            own = slice(head * size, (head + 1) * size)
            query = (turn(qkv_ref[:, own], cosine, sine) * size**-0.5).astype(b16)
            query_ref[:, own] = query
            _, probs = softmax_of(query, key, allowed)
            attended_ref[:, own] = dot(probs.astype(b16), value, ((1,), (0,))).astype(b16)


def attend_back_body(heads, kv_heads, d_att_ref, query_ref, key_ref, value_ref, cos_ref, sin_ref, row_ref, col_ref, out_ref):
    size = HEAD_DIM
    allowed = allowed_of(row_ref, col_ref)
    cosine, sine = cos_ref[...], sin_ref[...]
    for kv in range(kv_heads):
        own = slice(kv * size, (kv + 1) * size)
        key, value = key_ref[:, own], value_ref[:, own]
        d_key = d_value = 0.0
        for head in range(kv * heads // kv_heads, (kv + 1) * heads // kv_heads):
            own = slice(head * size, (head + 1) * size)
            query, d_att = query_ref[:, own], d_att_ref[:, own]
            ratio, probs = softmax_of(query, key, allowed)
            d_probs = dot(d_att, value, ((1,), (1,)))
            d_soft = probs * (d_probs - jnp.sum(probs * d_probs, axis=1, keepdims=True))
            d_scores = (d_soft * (1.0 - ratio * ratio)).astype(b16)
            d_query = dot(d_scores, key, ((1,), (0,))) * size**-0.5
            out_ref[:, own] = turn(d_query, cosine, -sine).astype(b16)
            d_key += dot(d_scores, query, ((0,), (0,)))
            d_value += dot(probs.astype(b16), d_att, ((0,), (0,)))
        at = heads * size + kv * size
        out_ref[:, at : at + size] = turn(d_key, cosine, -sine).astype(b16)
        at += kv_heads * size
        out_ref[:, at : at + size] = d_value.astype(b16)


def one_block(body, outs, *args):
    return pl.pallas_call(
        body,
        out_shape=outs,
        in_specs=[pl.BlockSpec(memory_space=pltpu.VMEM)] * len(args),
        out_specs=jax.tree.map(lambda _: pl.BlockSpec(memory_space=pltpu.VMEM), outs),
        compiler_params=pltpu.CompilerParams(vmem_limit_bytes=40 << 20),
        cost_estimate=pl.CostEstimate(flops=1000, bytes_accessed=1000, transcendentals=0),
    )(*args)


def dot(lhs, rhs, dims):
    return lax.dot_general(lhs, rhs, (dims, ((), ())), preferred_element_type=f32)


def swap(piece, axis):
    return lax.ppermute(piece, axis, [(0, 1), (1, 0)])


def hop(piece, step, n):
    return lax.ppermute(piece, "fsdp", [(d, d ^ step) for d in range(n)])


def gather_rows(own, n, checks=()):
    have, near = [own], hop(own, 1, n)
    bit = n // 2
    while bit > 1:
        new = [hop(piece, bit, n) for piece in have]
        if len(have) == 1:
            new = [after(new[0], near)]
        have = have + new
        bit //= 2
    even = jnp.concatenate(have)
    odd = jnp.concatenate([near] + [hop(piece, 1, n) for piece in have[1:]])
    return [jnp.concatenate([part, swap(part, "tp")]) for part in (even, odd)], have[1]


def after(value, *others):
    return lax.optimization_barrier((value, *others))[0]


def scatter_blocks(blocks, bit, n, serial=False, gates=None):
    marks = []
    while bit < n:
        keep = len(blocks) // 2
        marks.append(blocks[-1])
        came = [None] * keep
        order = sorted(range(keep), key=lambda k: keys_of(n)[k], reverse=True)
        for at, k in enumerate(order):
            piece = blocks[keep + k].astype(b16)
            if serial and bit == 1 and at:
                piece = after(piece, came[order[at - 1]], *gates.get(at, ()))
            came[k] = hop(piece, bit, n)
            if serial and bit == 1 and at == 1:
                marks[0] = came[k]
        blocks = [block + piece.astype(f32) for block, piece in zip(blocks, came)]
        bit *= 2
    return blocks[0], marks


def scatter_rows(product, sources, n):
    half = sources[0].shape[0] // 2
    rows = 2 * half // n
    take = lambda k: product(sources[k % 2][k // 2 * half : (k // 2 + 1) * half])
    far = [swap(take(k).astype(b16), "tp") for k in (3, 2)]
    odd = take(1) + far[0].astype(f32)
    even = take(0) + far[1].astype(f32)
    blocks = [part[k * rows : (k + 1) * rows] for part in (even, odd) for k in range(n // 2)]
    own, marks = scatter_blocks(blocks, 1, n)
    return own, [odd] + marks[1:]


def gather_group(own):
    across = swap(own, "ctx")
    beside = swap(jnp.concatenate([own, across]), "tp")
    rows = own.shape[0]
    return jnp.concatenate([own, beside[:rows], across, beside[rows:]])


def scatter_group(part):
    rows = part.shape[0] // 4
    b0, b1, b2, b3 = [part[k * rows : (k + 1) * rows] for k in range(4)]
    got = swap(jnp.concatenate([b1, b3]), "tp")
    return b0 + got[:rows] + swap((b2 + got[rows:]).astype(b16), "ctx").astype(f32)


def keys_of(n):
    order, bit = [0], n // 2
    while bit:
        order = order + [k ^ bit for k in order]
        bit //= 2
    return order


def tile_window(units, n):
    spans = [-(-(d + 1) * units // 128) - d * units // 128 for d in range(n)]
    return 128 * max(spans)


def natural(own, other, index, axis):
    first = jnp.where(index == 0, own, other)
    second = jnp.where(index == 0, other, own)
    return jnp.concatenate([first, second], axis=axis)


def local(
    n,
    tokens,
    cotangent,
    lengths,
    positions,
    query_weight,
    key_weight,
    value_weight,
    output_weight,
    gate_weight,
    up_weight,
    down_weight,
    gain_attn_in,
    gain_attn_out,
    gain_ffn_in,
    gain_ffn_out,
):
    me = lax.axis_index("fsdp")
    ctx = lax.axis_index("ctx")
    tp = lax.axis_index("tp")
    tok_rows, width = tokens.shape
    rows = tok_rows // 2
    head_size = HEAD_DIM
    d_rows = query_weight.shape[0]
    d_half = d_rows // 2
    q_cols = query_weight.shape[1] // 2
    k_cols = key_weight.shape[1] // 2
    q_local = q_cols // head_size
    kv_local = k_cols // head_size
    ff_local = gate_weight.shape[1]
    ff_own = ff_local // n

    starts = [
        c * tok_rows + t * rows for c in (ctx, 1 - ctx) for t in (tp, 1 - tp)
    ]
    packed = jnp.concatenate(
        [lax.dynamic_slice_in_dim(positions[0], start, rows) for start in starts]
    )
    segment, inner = placement_of(lengths[0], packed)
    angles = angles_of(inner, head_size)

    mine = lax.dynamic_slice_in_dim(tokens, tp * rows, rows)
    across = swap(mine, "ctx")
    beside = swap(across, "tp")
    seq_group = jnp.concatenate([tokens, across, beside])
    row_ids = jnp.arange(rows, dtype=jnp.int32)
    seq_ids = jnp.concatenate(
        [ctx * tok_rows + jnp.arange(tok_rows, dtype=jnp.int32), starts[2] + row_ids, starts[3] + row_ids]
    )
    pick = (packed[:, None] == seq_ids[None, :]).astype(b16)
    slot_in = dot(pick, seq_group, ((1,), (0,)))
    resid_in = slot_in[:rows]

    gain_row = jnp.concatenate([gain_attn_in, gain_attn_out, gain_ffn_in, gain_ffn_out])
    heads_cols = q_cols + 2 * k_cols
    gain_rows = -(-4 * d_rows // heads_cols)
    heads_own = jnp.concatenate(
        [
            lax.dynamic_slice_in_dim(query_weight, ctx * q_cols, q_cols, 1),
            lax.dynamic_slice_in_dim(key_weight, ctx * k_cols, k_cols, 1),
            lax.dynamic_slice_in_dim(value_weight, ctx * k_cols, k_cols, 1),
        ],
        axis=1,
    )
    heads_own = jnp.concatenate(
        [heads_own, jnp.pad(gain_row, (0, 16 * heads_cols - 4 * d_rows)).reshape(16, heads_cols)]
    )
    have = [(0, heads_own)]
    bit = n // 2
    while bit:
        have = have + [(k ^ bit, hop(piece, bit, n)) for k, piece in have]
        bit //= 2
    out_own = lax.dynamic_slice_in_dim(output_weight, ctx * q_cols, q_cols, 0).T
    out_own = after(out_own, have[1][1])
    out_weight = lax.all_gather(out_own, "fsdp", axis=0, tiled=True)
    qkv_weight = jnp.zeros((n, d_rows, heads_cols), b16)
    gains = jnp.zeros((n, gain_rows, heads_cols), b16)
    for k, piece in have:
        put = lambda whole, part: lax.dynamic_update_slice_in_dim(whole, part[None], me ^ k, 0)
        qkv_weight = put(qkv_weight, piece[:d_rows])
        gains = put(gains, piece[d_rows : d_rows + gain_rows])
    qkv_weight = qkv_weight.reshape(width, heads_cols)
    gains = gains.reshape(n, gain_rows * heads_cols)[:, : 4 * d_rows]
    gains = gains.reshape(n, 4, d_rows).transpose(1, 0, 2).reshape(4, width).astype(f32)

    window = tile_window(ff_own, n)
    first = lambda device: (device * ff_own) & -128
    unit = first(me) + jnp.arange(window, dtype=jnp.int32)
    valid = ((unit >= me * ff_own) & (unit < (me + 1) * ff_own))[None]

    def to_units(weights):
        halves = [lax.dynamic_slice_in_dim(weight, ctx * d_half, d_half) for weight in weights]
        own = jnp.stack(
            [
                jnp.concatenate([half[:, first(d) : first(d) + window] for half in halves], axis=1)
                for d in range(n)
            ]
        )
        return lax.all_to_all(own, "fsdp", 0, 0, tiled=True)

    def both_halves(half, other):
        whole = jnp.zeros((n, 2, *half.shape[1:]), b16)
        whole = lax.dynamic_update_slice_in_dim(whole, half[:, None], ctx, 1)
        whole = lax.dynamic_update_slice_in_dim(whole, other[:, None], 1 - ctx, 1)
        return whole.reshape(width, half.shape[2])

    far_piece = have[n // 2 - 1][1]
    gu_half = to_units([after(weight, far_piece) for weight in (gate_weight, up_weight)])

    normed_attn = rms_scale(slot_in, gains[0]).astype(b16)
    qkv = dot(normed_attn, qkv_weight, ((1,), (0,)))
    all_rows = 2 * tok_rows
    cosine, sine = jnp.cos(angles), jnp.sin(angles)
    places = jnp.stack([segment, inner])
    held = lambda cols: jax.ShapeDtypeStruct((all_rows, cols), b16)
    attended, queries, keys, values = one_block(
        functools.partial(attend_body, q_local, kv_local),
        [held(q_cols), held(q_cols), held(k_cols), held(k_cols)],
        qkv,
        cosine,
        sine,
        places.T,
        places,
    )
    attn_out = scatter_group(dot(attended, out_weight, ((1,), (1,))))
    middle = resid_in + rms_scale(attn_out, gains[1])

    normed_own = rms_scale(middle, gains[2]).astype(b16)
    gu_other = swap(after(gu_half, attn_out), "ctx")
    normed_ffn, mark = gather_rows(normed_own, n)
    down_half = to_units([after(down_weight.T, mark)])
    down_other = swap(after(down_half, gu_other), "ctx")
    gu_full = both_halves(gu_half, gu_other)
    down_full = both_halves(down_half, down_other)
    gates_and_ups = [dot(part, gu_full, ((1,), (0,))) for part in normed_ffn]
    acts = [(part[:, :window], part[:, window:]) for part in gates_and_ups]
    hidden = [jnp.where(valid, glu_apply(*pair), 0.0).astype(b16) for pair in acts]
    ffn_out, _ = scatter_rows(lambda part: dot(part, down_full, ((1,), (1,))), hidden, n)
    block_own = (middle + rms_scale(ffn_out, gains[3])).astype(b16)
    block_out = natural(block_own, swap(block_own, "tp"), tp, 0)

    d_out = lax.dynamic_slice_in_dim(cotangent, tp * rows, rows).astype(f32)
    d_ffn_raw, gain_four_term = norm_back(ffn_out, gains[3], d_out)
    d_ffn_out, _ = gather_rows(d_ffn_raw.astype(b16), n)
    d_pairs = [
        jax.vjp(glu_apply, *pair)[1](dot(part, down_full, ((1,), (0,))))
        for pair, part in zip(acts, d_ffn_out)
    ]
    d_pairs = [[jnp.where(valid, part, 0.0).astype(b16) for part in pair] for pair in d_pairs]
    d_normed_ffn, marks = scatter_rows(
        lambda part: dot(part, gu_full, ((1,), (1,))),
        [jnp.concatenate(pair, axis=1) for pair in d_pairs],
        n,
    )

    def halves(terms):
        terms = terms.reshape(n, 2, d_half, window)
        send = lax.dynamic_index_in_dim(terms, 1 - ctx, 1, keepdims=False).astype(b16)
        return send, lax.dynamic_index_in_dim(terms, ctx, 1, keepdims=False)

    hidden, d_ffn_out, normed_ffn = [
        jnp.concatenate([after(part, marks[0]) for part in parts])
        for parts in (hidden, d_ffn_out, normed_ffn)
    ]
    d_gate, d_up = [jnp.concatenate(parts) for parts in zip(*d_pairs)]
    down_send, down_keep = halves(dot(d_ffn_out, hidden, ((0,), (0,))))
    late_normed = after(normed_ffn, marks[-1], down_send)
    gate_send, gate_keep = halves(dot(late_normed, d_gate, ((0,), (0,))))
    up_send, up_keep = halves(dot(after(late_normed, gate_send), d_up, ((0,), (0,))))
    down_got, gate_got = swap(down_send, "ctx"), swap(gate_send, "ctx")

    def to_owners(keeps, gots, gate):
        gots = [after(got, gate) for got in gots]
        low = [(keep + got.astype(f32)).astype(b16) for keep, got in zip(keeps, gots)]
        return lax.all_to_all(jnp.concatenate(low, axis=2), "fsdp", 0, 0, tiled=True)

    def columns_joined(whole):
        period = 128 // math.gcd(ff_own, 128)
        tiles = period * ff_own // 128
        parts = whole.reshape(n // period, period, *whole.shape[1:]).astype(f32)
        runs = []
        for tile in range(tiles):
            holds = [
                d
                for d in range(period)
                if d * ff_own < (tile + 1) * 128 and (d + 1) * ff_own > tile * 128
            ]
            if runs and runs[-1][0] == holds and len(holds) == 1:
                runs[-1][2] = tile + 1
            else:
                runs.append([holds, tile, tile + 1])
        pieces = [
            sum(parts[:, d, ..., a * 128 - first(d) : b * 128 - first(d)] for d in holds)
            for holds, a, b in runs
        ]
        joined = jnp.concatenate(pieces, axis=-1)
        return joined.transpose(1, 0, 2).reshape(whole.shape[1], ff_local)

    d_normed_ffn = after(d_normed_ffn, down_got, gate_send, up_send)
    d_middle_part, gain_three_term = norm_back(middle, gains[2], d_normed_ffn)
    d_middle = d_out + d_middle_part
    d_attn_raw, gain_two_term = norm_back(attn_out, gains[1], d_middle)
    d_attn_out = gather_group(d_attn_raw.astype(b16))
    up_got = swap(after(up_send, d_attn_out), "ctx")
    down_rows = to_owners([down_keep], [down_got], d_normed_ffn)
    d_attended = dot(d_attn_out, out_weight, ((1,), (0,))).astype(b16)
    d_qkv = one_block(
        functools.partial(attend_back_body, q_local, kv_local),
        held(q_cols + 2 * k_cols),
        d_attended,
        queries,
        keys,
        values,
        cosine,
        sine,
        places.T,
        places,
    )
    d_normed_part = dot(d_qkv, qkv_weight, ((1,), (1,)))
    d_normed_attn = scatter_group(d_normed_part)
    resid_part, gain_one_term = norm_back(resid_in, gains[0], d_normed_attn)
    slot_grad = gather_group((d_middle + resid_part).astype(b16))
    unpick = (
        (ctx * tok_rows + jnp.arange(tok_rows, dtype=jnp.int32))[:, None] == packed[None, :]
    ).astype(b16)
    tokens_grad = dot(unpick, slot_grad, ((1,), (0,))).astype(b16)

    down_weight_grad = columns_joined(down_rows).T
    attn_terms = [
        dot(normed_attn, d_qkv, ((0,), (0,))).reshape(n, d_rows, -1),
        dot(d_attn_out, attended, ((0,), (0,))).reshape(n, d_rows, -1),
    ]
    attn_rows, marks = scatter_blocks(
        [
            jnp.concatenate(
                [lax.dynamic_index_in_dim(terms, me ^ k, 0, keepdims=False) for terms in attn_terms],
                axis=1,
            )
            for k in keys_of(n)
        ],
        1,
        n,
        serial=True,
        gates={1: [down_rows], 2: [down_weight_grad]},
    )
    gu_rows = after(to_owners([gate_keep, up_keep], [gate_got, up_got], marks[0]), attn_rows)
    gate_rows, up_rows = gu_rows[..., :window], gu_rows[..., window:]
    gate_weight_grad = columns_joined(gate_rows)
    up_weight_grad = columns_joined(up_rows)
    attn_rows = attn_rows.reshape(2, d_half, -1)
    attn_own = lax.dynamic_index_in_dim(attn_rows, ctx, 0, keepdims=False)
    attn_other = swap(
        lax.dynamic_index_in_dim(attn_rows, 1 - ctx, 0, keepdims=False).astype(b16), "ctx"
    )
    attn_other = after(attn_other, gate_weight_grad, up_weight_grad)
    edges = [0, q_cols, q_cols + k_cols, q_cols + 2 * k_cols, 2 * q_cols + 2 * k_cols]
    attn_grads = [
        natural(attn_own[:, a:b].astype(f32), attn_other[:, a:b].astype(f32), ctx, 1)
        for a, b in zip(edges[:-1], edges[1:])
    ]

    gain_terms = jnp.stack([gain_one_term, gain_two_term, gain_three_term, gain_four_term])
    gain_terms = gain_terms + swap(gain_terms, "tp")
    gain_terms = gain_terms.reshape(4, n, 2, d_half).transpose(1, 2, 0, 3)
    gain_terms = lax.dynamic_index_in_dim(gain_terms, ctx, 1, keepdims=False) + swap(
        lax.dynamic_index_in_dim(gain_terms, 1 - ctx, 1, keepdims=False), "ctx"
    )
    gain_rows = jnp.stack(
        [lax.dynamic_index_in_dim(gain_terms, me ^ k, 0, keepdims=False) for k in keys_of(n)]
    )
    gain_rows = after(gain_rows, attn_rows)
    bit = 1
    while bit < n:
        keep = gain_rows.shape[0] // 2
        gain_rows = gain_rows[:keep] + hop(gain_rows[keep:], bit, n)
        bit *= 2
    gain_rows = gain_rows[0]
    return (
        block_out,
        tokens_grad,
        attn_grads[0],
        attn_grads[1],
        attn_grads[2],
        attn_grads[3].T,
        gate_weight_grad,
        up_weight_grad,
        down_weight_grad,
        gain_rows[0],
        gain_rows[1],
        gain_rows[2],
        gain_rows[3],
    )


def solution(mesh):
    in_specs = (
        P(("fsdp", "ctx"), None),
        P(("fsdp", "ctx"), None),
        P("fsdp", None),
        P("fsdp", None),
        P("fsdp", "tp"),
        P("fsdp", "tp"),
        P("fsdp", "tp"),
        P("tp", "fsdp"),
        P("fsdp", "tp"),
        P("fsdp", "tp"),
        P("tp", "fsdp"),
        P("fsdp"),
        P("fsdp"),
        P("fsdp"),
        P("fsdp"),
    )
    out_specs = (
        P(("fsdp", "ctx"), None),
        P(("fsdp", "ctx"), None),
        P(("fsdp", "ctx"), "tp"),
        P(("fsdp", "ctx"), "tp"),
        P(("fsdp", "ctx"), "tp"),
        P("tp", ("fsdp", "ctx")),
        P(("fsdp", "ctx"), "tp"),
        P(("fsdp", "ctx"), "tp"),
        P("tp", ("fsdp", "ctx")),
        P(("fsdp", "ctx")),
        P(("fsdp", "ctx")),
        P(("fsdp", "ctx")),
        P(("fsdp", "ctx")),
    )
    step = functools.partial(local, mesh.shape["fsdp"])
    return jax.shard_map(step, mesh=mesh, in_specs=in_specs, out_specs=out_specs, check_vma=False)
```
